32 devices in a mesh: ctx: 16 (over z, y, x), head: 2 (over core).
Axes of the slice: x: 2, y: 2, z: 4, core: 2. Of those that a mesh axis runs over, the one named last changes fastest.
Arguments:
- queries: bfloat16 [2, 4096, 2048], P(None, 'ctx', 'head'), may hold values from -6 to 6
- key_vectors: bfloat16 [2, 4096, 2048], P(None, 'ctx', 'head'), may hold values from -0.4 to 0.4
- value_vectors: bfloat16 [2, 4096, 2048], P(None, 'ctx', 'head'), may hold values from -6 to 6
- log_decay: float32 [16, 2, 4096], P('head', None, 'ctx'), may hold values from -1 to 0
- ridge_shift: float32 [16], P('head'), may hold values from 0.25 to 4
- norm_gain: float32 [2048], P('head'), may hold values from 0.1 to 1.9
- out_weight: bfloat16 [2048, 4096], P(None, 'head'), may hold values from -0.125 to 0.125
Outputs:
- mixed: bfloat16 [2, 4096, 4096], P(None, 'ctx', 'head')
The draws below stay inside these ranges and needn't reach their ends.
All inputs are finite; a program needn't handle non-finite values.
Results may differ from the reference program's by a relative error of at most 0.007.
Values may be sent and summed in bfloat16 or wider, within the bound.
No kernel may reach another device: no remote copies, remote signals or barrier semaphores. Data moves between devices by JAX's collectives and lax.ppermute only.
A program may use at most 128 MiB of HBM per device.

```python
import math
import jax
import jax.numpy as jnp
from jax import lax

D = 4096
HEAD_COUNT = 16
DK = 128
DV = 128
GROUP = 256
ITERS = 2
TOK_DEV = 512
SEQ = 8192
HALFSEQ = 4096
N_CTX = 16


anchor_count = 9


direction_count = 8


key_limit = 0.3984375


def draw_log_decay(key, part):
    parallel_lanes = jax.random.split(jax.random.fold_in(key, 11), 6)
    full_shape = (HEAD_COUNT, 2, HALFSEQ)
    quick = jax.random.uniform(parallel_lanes[0], (HEAD_COUNT, 1, 1)) < 0.5
    head_factor = jnp.exp(jax.random.uniform(parallel_lanes[1], (HEAD_COUNT, 1, 1), minval=-0.7, maxval=0.7))
    baseline_decay = jnp.where(quick, 1.0 / 40.0, 0.3 / SEQ) * head_factor
    group_blocks = HALFSEQ // GROUP
    group_multiplier = jnp.exp(jax.random.uniform(parallel_lanes[2], (HEAD_COUNT, 2, group_blocks, 1), minval=-0.7, maxval=0.7))
    group_multiplier = jnp.broadcast_to(group_multiplier, (HEAD_COUNT, 2, group_blocks, GROUP)).reshape(full_shape)
    element_multiplier = jax.random.uniform(parallel_lanes[3], full_shape, minval=0.5, maxval=1.5)
    places = jax.random.randint(parallel_lanes[4], (2,), 0, 2 * HALFSEQ)
    flat_index = jnp.arange(2 * HALFSEQ).reshape(1, 2, HALFSEQ)
    selected_entries = jnp.any(flat_index[..., None] == places, axis=-1)
    spike_penalty = jnp.log(jax.random.uniform(parallel_lanes[5], (HEAD_COUNT, 1, 1), minval=0.5, maxval=0.8))
    spike_events = jnp.where(selected_entries, spike_penalty, 0.0)
    return (spike_events - baseline_decay * group_multiplier * element_multiplier).astype(jnp.float32)


def draw_key_vectors(key, part):
    lanes = jax.random.split(jax.random.fold_in(key, 23), 4)
    block_len = TOK_DEV // 2
    index_row = jnp.arange(HALFSEQ, dtype=jnp.int32)
    back_row = SEQ - (index_row // block_len + 1) * block_len + index_row % block_len
    positions = jnp.stack([index_row, back_row], axis=0)
    spans = anchor_count - 1
    segment = positions * spans // SEQ
    fraction = (positions * spans - segment * SEQ).astype(jnp.float32) / SEQ
    anchors = jnp.arange(anchor_count, dtype=jnp.int32)
    blend = jnp.where(anchors == segment[..., None], 1.0 - fraction[..., None], 0.0)
    blend = blend + jnp.where(anchors == segment[..., None] + 1, fraction[..., None], 0.0)
    directions = jax.random.normal(lanes[0], (HEAD_COUNT, anchor_count, direction_count, DK), jnp.float32)
    amplitude = jnp.exp(jax.random.uniform(lanes[1], (HEAD_COUNT, direction_count), minval=jnp.log(0.15), maxval=jnp.log(0.45)))
    coef_shape = (2, HALFSEQ, HEAD_COUNT, direction_count)
    noise_shape = (2, HALFSEQ, HEAD_COUNT, DK)
    coefficients = jax.random.normal(lanes[2], coef_shape, jnp.float32)
    noise = jax.random.normal(lanes[3], noise_shape, jnp.float32)
    coefficients = coefficients * amplitude
    weighted = blend[:, :, None, :, None] * coefficients[:, :, :, None, :]
    shared = jnp.einsum('pthar,hard->pthd', weighted, directions)
    keys_now = jnp.clip(0.09 * (0.7 * noise + shared), -key_limit, key_limit)
    return keys_now.reshape(2, HALFSEQ, HEAD_COUNT * DK).astype(jnp.bfloat16)


def levels(rng, extent, shards, low, high):
    def one(dim, blocks):
        steps = jax.random.uniform(jax.random.fold_in(jax.random.fold_in(rng, 6), dim), (blocks,), jnp.float32, low / len(shards), high / len(shards))
        return jnp.repeat(jnp.exp(steps), extent[dim] // blocks).reshape((-1,) + (1,) * (len(extent) - dim - 1))

    level = one(*shards[0])
    for cut in shards[1:]:
        level = level * one(*cut)
    return level


def gaussian(own_key, extent, deviation, limit, pieces=(), kind=jnp.bfloat16):
    values = deviation * jax.random.normal(own_key, extent, jnp.float32)
    if pieces:
        values = values * levels(own_key, extent, pieces, -0.22, 0.18)
    return jnp.clip(values, -limit, limit).astype(kind)


def setup_inputs(seed: int = 0) -> dict:
    splits = jax.random.split(jax.random.key(seed), 8)
    queries = gaussian(splits[0], (2, HALFSEQ, HEAD_COUNT * DK), 1.0, 6.0, ((1, 16), (2, 2)))
    key_vectors = draw_key_vectors(jax.random.fold_in(splits[7], 71), 0)
    value_vectors = gaussian(splits[2], (2, HALFSEQ, HEAD_COUNT * DV), 1.0, 6.0, ((1, 16), (2, 2)))
    log_decay = draw_log_decay(jax.random.fold_in(splits[7], 71), 0)
    ridge_shift = jnp.clip(jnp.exp(math.log(4.0) - 2.7725887 * jax.random.uniform(splits[4], (HEAD_COUNT,), jnp.float32) ** levels(splits[4], (HEAD_COUNT,), ((0, 2),), -0.2, 0.2)), 0.25, 4.0)
    norm_gain = jnp.clip(1.0 + 0.18 * jax.random.normal(splits[5], (HEAD_COUNT * DV,), jnp.float32), 0.1, 1.9)
    out_weight = gaussian(splits[6], (HEAD_COUNT * DV, D), (HEAD_COUNT * DV) ** -0.5, 0.125, ((1, 2),))
    return dict(queries=queries, key_vectors=key_vectors, value_vectors=value_vectors, log_decay=log_decay, ridge_shift=ridge_shift, norm_gain=norm_gain, out_weight=out_weight)


exact_mode = lax.Precision.HIGHEST
norm_epsilon = 1e-06
solve_epsilon = 1e-06

def decay_masks(log_rates):
    cumulative = jnp.cumsum(log_rates, axis=-1)
    width_now = log_rates.shape[-1]
    differ = cumulative[..., :, None] - cumulative[..., None, :]
    lower_part = jnp.arange(width_now)[:, None] >= jnp.arange(width_now)[None, :]
    within = jnp.where(lower_part, jnp.exp(jnp.minimum(differ, 0.0)), 0.0)
    return (cumulative, within)

def group_state(key_rows, value_rows, cumulative):
    weights = jnp.exp(cumulative[..., -1:] - cumulative)[..., None]
    key_gram = jnp.einsum('...sd,...se->...de', key_rows * weights, key_rows, precision=exact_mode)
    value_key = jnp.einsum('...se,...sd->...ed', value_rows * weights, key_rows, precision=exact_mode)
    return (cumulative[..., -1], key_gram, value_key)

def group_outputs(query_rows, key_rows, value_rows, cumulative, within, key_gram, value_key, ridge_term):
    entering = jnp.exp(cumulative)[..., None]

    def operator(vectors):
        scores = jnp.einsum('...cd,...sd->...cs', vectors, key_rows, precision=exact_mode) * within
        carried = jnp.einsum('...cd,...de->...ce', vectors, key_gram, precision=exact_mode)
        local_part = jnp.einsum('...cs,...sd->...cd', scores, key_rows, precision=exact_mode)
        return entering * carried + local_part + ridge_term * vectors
    solution = jnp.zeros_like(query_rows)
    residual = query_rows
    direction = query_rows
    norm_now = lax.optimization_barrier(jnp.sum(residual * residual, axis=-1, keepdims=True))
    for iteration in range(ITERS):
        product = operator(direction)
        step_size = norm_now / (lax.optimization_barrier(jnp.sum(direction * product, axis=-1, keepdims=True)) + solve_epsilon)
        solution = solution + step_size * direction
        residual = residual - step_size * product
        if iteration + 1 < ITERS:
            norm_next = lax.optimization_barrier(jnp.sum(residual * residual, axis=-1, keepdims=True))
            direction = residual + norm_next / (norm_now + solve_epsilon) * direction
            norm_now = norm_next
    scores = jnp.einsum('...cd,...sd->...cs', solution, key_rows, precision=exact_mode) * within
    carried = jnp.einsum('...cd,...ed->...ce', solution, value_key, precision=exact_mode)
    return entering * carried + jnp.einsum('...cs,...se->...ce', scores, value_rows, precision=exact_mode)

def finish(readout, gain_rows):
    scale_rows = lax.rsqrt(lax.optimization_barrier(jnp.mean(readout * readout, axis=-1, keepdims=True)) + norm_epsilon)
    return (readout * scale_rows * gain_rows).astype(jnp.bfloat16)

def to_sequence(packed):
    block_len = TOK_DEV // 2
    columns = packed.shape[-1]
    mirror = packed[1].reshape(N_CTX, block_len, columns)[::-1].reshape(HALFSEQ, columns)
    return jnp.concatenate([packed[0], mirror], axis=0)

def to_layout(ordered):
    block_len = TOK_DEV // 2
    columns = ordered.shape[-1]
    front_half = ordered[:HALFSEQ]
    mirror = ordered[HALFSEQ:].reshape(N_CTX, block_len, columns)[::-1].reshape(HALFSEQ, columns)
    return jnp.stack([front_half, mirror], axis=0)

def reference(queries, key_vectors, value_vectors, log_decay, ridge_shift, norm_gain, out_weight):
    group_total = SEQ // GROUP

    def heads_view(packed, feature_width):
        ordered = to_sequence(packed).astype(jnp.float32)
        return ordered.reshape(group_total, GROUP, HEAD_COUNT, feature_width).transpose(0, 2, 1, 3)
    query_seq = heads_view(queries, DK)
    key_seq = heads_view(key_vectors, DK)
    value_seq = heads_view(value_vectors, DV)
    rate_seq = to_sequence(log_decay.transpose(1, 2, 0)).reshape(group_total, GROUP, HEAD_COUNT).transpose(0, 2, 1)
    ridge_term = ridge_shift[:, None, None]
    gain_rows = norm_gain.reshape(HEAD_COUNT, 1, DV)

    def advance(carry_state, inputs_now):
        key_gram, value_key = carry_state
        query_now, key_now, value_now, rates_now = inputs_now
        cumulative, within = decay_masks(rates_now)
        readout = group_outputs(query_now, key_now, value_now, cumulative, within, key_gram, value_key, ridge_term)
        totals, group_gram, group_memory = group_state(key_now, value_now, cumulative)
        fading = jnp.exp(totals)[:, None, None]
        return ((fading * key_gram + group_gram, fading * value_key + group_memory), finish(readout, gain_rows))
    initial = (jnp.zeros((HEAD_COUNT, DK, DK), jnp.float32), jnp.zeros((HEAD_COUNT, DV, DK), jnp.float32))
    _, normed = lax.scan(advance, initial, (query_seq, key_seq, value_seq, rate_seq))
    normed = normed.transpose(0, 2, 1, 3).reshape(SEQ, HEAD_COUNT * DV)
    mixed_out = jnp.dot(normed, out_weight, preferred_element_type=jnp.float32).astype(jnp.bfloat16)
    return to_layout(mixed_out)
```

```python
import functools

import jax
import jax.numpy as jnp
from jax import lax
from jax.experimental import pallas as pl
from jax.experimental.pallas import tpu as pltpu
from jax.sharding import PartitionSpec as P

DK = 128
DV = 128
GROUP = 256
PAIR = 2 * DK
TAIL = 16
ROWS_G = 2 * DK + TAIL
ROWS_M = 4 * DK
norm_epsilon = 1e-06
solve_epsilon = 1e-06

F32 = jnp.float32
BF16 = jnp.bfloat16
MIB = 1024 * 1024


def iota2(shape, dim):
    return lax.broadcasted_iota(jnp.int32, shape, dim)


def dot(a, b):
    return lax.dot_general(a, b, (((1,), (0,)), ((), ())), preferred_element_type=F32)


def dot_nt(a, b):
    return lax.dot_general(a, b, (((1,), (1,)), ((), ())), preferred_element_type=F32)


def split3(x):
    high = x.astype(BF16).astype(F32)
    middle = (x - high).astype(BF16).astype(F32)
    low = (x - high - middle).astype(BF16).astype(F32)
    return (high, middle, low)


def square_lower():
    return iota2((DK, DK), 0) >= iota2((DK, DK), 1)


def states_kernel(pairs, rate_ref, key_ref, value_ref, gram_out, memory_out):
    rows = 4 * pairs
    rates = jnp.concatenate([rate_ref[h] for h in range(2 * pairs)], axis=0)
    parts = jnp.concatenate(split3(rates), axis=0).astype(BF16)
    upper = (iota2((GROUP, GROUP), 0) <= iota2((GROUP, GROUP), 1)).astype(BF16)
    sums = dot(parts, upper)
    cumulative = sums[:rows] + sums[rows : 2 * rows] + sums[2 * rows :]
    whole = dot(parts, jnp.ones((GROUP, DK), BF16))
    totals = whole[:rows] + whole[rows : 2 * rows] + whole[2 * rows :]
    weights = jnp.exp(
        jnp.minimum(jnp.concatenate([totals, totals], axis=1) - cumulative, 0.0)
    )
    logs = split3(totals)
    lower = square_lower()
    diagonal = iota2((DK, DK), 0) == iota2((DK, DK), 1)
    for pair in range(pairs):
        tail = []
        for row in range(2):
            grams = []
            for odd in range(2):
                head = 2 * pair + odd
                index = 2 * head + row
                columns = pl.ds(head * DK, DK)
                keys = key_ref[row, :, columns]
                values = value_ref[row, :, columns]
                turned = keys.astype(F32).T * weights[index : index + 1, :]
                product = dot(turned.astype(BF16), jnp.concatenate([keys, values], axis=1))
                grams.append(product[:, :DK])
                memory_out[pair, pl.ds((2 * row + odd) * DK, DK), :] = product[:, DK:].astype(BF16)
            folded = jnp.where(lower, grams[0], grams[1])
            gram_out[pair, pl.ds(row * DK, DK), :] = folded.astype(BF16)
            tail.append(jnp.sum(jnp.where(diagonal, grams[1], 0.0), axis=0, keepdims=True))
        for row in range(2):
            for odd in range(2):
                index = 2 * (2 * pair + odd) + row
                tail += [part[index : index + 1, :] for part in logs]
        tail.append(jnp.zeros((2, DK), F32))
        gram_out[pair, pl.ds(2 * DK, TAIL), :] = jnp.concatenate(tail, axis=0).astype(BF16)


def read_logs(ref, item):
    tail = ref[item, pl.ds(ref.shape[1] - TAIL, TAIL), :].astype(F32)

    def one(start):
        return tail[start : start + 1] + tail[start + 1 : start + 2] + tail[start + 2 : start + 3]

    return {("F", 0): one(2), ("F", 1): one(5), ("B", 0): one(8), ("B", 1): one(11)}


def pick(flag, a, b):
    return jnp.where(flag, a, b)


def add_logs(logs, flags):
    total = jnp.zeros((1, DK), F32)
    for log, flag in zip(logs, flags):
        total = total + jnp.where(flag, log, 0.0)
    return total


class Gram:
    rows = DK

    @staticmethod
    def load(ref, item, which):
        return ref[item, pl.ds(which * DK, DK), :].astype(F32)

    @staticmethod
    def weight(pair_of_weights):
        return jnp.where(square_lower(), pair_of_weights[0], pair_of_weights[1])

    @staticmethod
    def load_tail(ref, item, which):
        start = ref.shape[1] - TAIL + which
        return ref[item, pl.ds(ref.shape[1] - TAIL, TAIL), :].astype(F32)[which : which + 1]


class Memory:
    rows = 2 * DK

    @staticmethod
    def load(ref, item, which):
        return ref[item, pl.ds(which * 2 * DK, 2 * DK), :].astype(F32)

    @staticmethod
    def weight(pair_of_weights):
        even = jnp.broadcast_to(pair_of_weights[0], (DK, DK))
        odd = jnp.broadcast_to(pair_of_weights[1], (DK, DK))
        return jnp.concatenate([even, odd], axis=0)


def load_all(kind, ref, item, which):
    body = kind.load(ref, item, which)
    if kind is Gram:
        return (body, Gram.load_tail(ref, item, which))
    return (body,)


def scaled(kind, value, weights):
    out = (value[0] * kind.weight(weights),)
    if kind is Gram:
        out += (value[1] * weights[1],)
    return out


def plus(a, b):
    return tuple(x + y for x, y in zip(a, b))


def log_rows(logs):
    rows = []
    for name in ("F", "B"):
        for odd in range(2):
            rows += list(split3(logs[name, odd]))
    return rows


def write(kind, ref, item, values, logs):
    for which, value in enumerate(values):
        ref[item, pl.ds(which * kind.rows, kind.rows), :] = value[0].astype(BF16)
    if kind is Gram:
        tails = [value[1] for value in values]
        tails += [jnp.zeros((1, DK), F32)] * (2 - len(tails))
        tails += log_rows(logs) if logs is not None else [jnp.zeros((12, DK), F32)]
        tails.append(jnp.zeros((2, DK), F32))
        ref[item, pl.ds(ref.shape[1] - TAIL, TAIL), :] = jnp.concatenate(tails, axis=0).astype(BF16)


def emit(kind, item, front, back, logs, last_bit, outs):
    if last_bit is None:
        write(kind, outs[0], item, [front, back], logs)
        return
    upper = last_bit == 1
    weights = [pick(upper, jnp.exp(logs["B", odd]), 1.0) for odd in range(2)]
    merged = scaled(kind, front, weights)
    merged = plus(merged, tuple(jnp.where(upper, x, 0.0) for x in back))
    write(kind, outs[0], item, [merged], logs)
    write(kind, outs[1], item, [front], logs)


def plane_kernel(kind, members, items, bit_next, where_ref, *refs):
    state_refs, log_refs, outs = refs[:members], refs[members : 2 * members], refs[2 * members :]
    place = where_ref[0]
    last_bit = None if bit_next is None else (where_ref[1] >> bit_next) & 1
    order = [place ^ d for d in range(members)]
    for item in range(items):
        logs = [read_logs(ref, item) for ref in log_refs]
        front = back = None
        for d in range(members):
            after = [order[e] > order[d] for e in range(members)]
            before = [order[e] < order[d] for e in range(members)]
            front_weights = [
                jnp.exp(add_logs([log["F", odd] for log in logs], after)) for odd in range(2)
            ]
            back_weights = [
                jnp.exp(add_logs([log["B", odd] for log in logs], before)) for odd in range(2)
            ]
            f = scaled(kind, load_all(kind, state_refs[d], item, 0), front_weights)
            b = scaled(kind, load_all(kind, state_refs[d], item, 1), back_weights)
            front = f if front is None else plus(front, f)
            back = b if back is None else plus(back, b)
        total = {key: sum(log[key] for log in logs[1:]) + logs[0][key] for key in logs[0]}
        emit(kind, item, front, back, total, last_bit, outs)


def step_kernel(kind, items, bit, bit_next, where_ref, own_ref, got_ref, own_log, got_log, *outs):
    upper = ((where_ref[1] >> bit) & 1) == 1
    last_bit = None if bit_next is None else (where_ref[1] >> bit_next) & 1
    for item in range(items):
        mine, theirs = read_logs(own_log, item), read_logs(got_log, item)
        up = {key: pick(upper, mine[key], theirs[key]) for key in mine}
        low = {key: pick(upper, theirs[key], mine[key]) for key in mine}
        sides = []
        for which, name, far, near in ((0, "F", low, up), (1, "B", up, low)):
            decay = [jnp.exp(near[name, odd]) for odd in range(2)]
            far_is_own = upper if which == 1 else jnp.logical_not(upper)
            own_weights = [pick(far_is_own, w, 1.0) for w in decay]
            got_weights = [pick(far_is_own, 1.0, w) for w in decay]
            sides.append(
                plus(
                    scaled(kind, load_all(kind, own_ref, item, which), own_weights),
                    scaled(kind, load_all(kind, got_ref, item, which), got_weights),
                )
            )
        total = {key: mine[key] + theirs[key] for key in mine}
        emit(kind, item, sides[0], sides[1], total, last_bit, outs)


def entering_kernel(kind, members, items, steps, where_ref, *refs):
    refs = list(refs)

    def take(count):
        taken = refs[:count]
        del refs[:count]
        return taken

    state_refs, log_refs = take(members), take(members)
    got_refs, got_logs = take(steps), take(steps)
    (keep_ref,), (own_log,) = take(1), take(1)
    outs = refs
    place = where_ref[0]
    order = [place ^ d for d in range(members)]
    for item in range(items):
        zero = jnp.zeros((1, DK), F32)
        late_front, late_back = [zero, zero], [zero, zero]
        base_front = base_back = None
        for step in range(steps):
            upper = ((where_ref[1] >> step) & 1) == 1
            theirs = read_logs(got_logs[step], item)
            front = load_all(kind, got_refs[step], item, 0)
            front_weights = [pick(upper, jnp.exp(late_front[odd]), 0.0) for odd in range(2)]
            add_front = scaled(kind, front, front_weights)
            base_front = add_front if base_front is None else plus(base_front, add_front)
            if step < steps - 1:
                back = load_all(kind, got_refs[step], item, 1)
                back_weights = [pick(upper, 0.0, jnp.exp(late_back[odd])) for odd in range(2)]
                add_back = scaled(kind, back, back_weights)
                base_back = add_back if base_back is None else plus(base_back, add_back)
                for odd in range(2):
                    late_front[odd] = late_front[odd] + pick(upper, theirs["F", odd], 0.0)
                    late_back[odd] = late_back[odd] + pick(upper, 0.0, theirs["B", odd])
            else:
                mine = read_logs(own_log, item)
                keep_weights = [
                    jnp.exp(late_back[odd] + pick(upper, 0.0, theirs["F", odd] + theirs["B", odd]))
                    for odd in range(2)
                ]
                got_weights = [
                    jnp.exp(late_back[odd] + pick(upper, mine["F", odd], 0.0)) for odd in range(2)
                ]
                add_back = plus(
                    scaled(kind, load_all(kind, keep_ref, item, 0), keep_weights),
                    scaled(kind, front, got_weights),
                )
                base_back = add_back if base_back is None else plus(base_back, add_back)
        logs = [read_logs(ref, item) for ref in log_refs]
        for target in range(members):
            here = order[target]
            results = []
            for which, name, base in ((0, "F", base_front), (1, "B", base_back)):

                def ahead(a, b):
                    return a < b if which == 0 else a > b

                total = scaled(
                    kind,
                    base,
                    [
                        jnp.exp(
                            add_logs([log[name, odd] for log in logs], [ahead(o, here) for o in order])
                        )
                        for odd in range(2)
                    ],
                )
                for source in range(members):
                    if source == target:
                        continue
                    there = order[source]
                    between = [
                        jnp.logical_and(ahead(there, o), ahead(o, here)) for o in order
                    ]
                    weights = [
                        pick(
                            ahead(there, here),
                            jnp.exp(add_logs([log[name, odd] for log in logs], between)),
                            0.0,
                        )
                        for odd in range(2)
                    ]
                    total = plus(
                        total,
                        scaled(kind, load_all(kind, state_refs[source], item, which), weights),
                    )
                results.append(total)
            write(kind, outs[target], item, results, None)


def local_kernel(rate_ref, query_ref, key_ref, value_ref, masked_out, product_out, column_out):
    rates = jnp.concatenate([rate_ref[h] for h in range(2)], axis=0)
    rates = jnp.concatenate([rates, jnp.zeros((4, GROUP), F32)], axis=0)
    parts = jnp.concatenate(split3(rates) + (jnp.zeros((8, GROUP), F32),), axis=0).astype(BF16)
    upper = (iota2((GROUP, GROUP), 0) <= iota2((GROUP, GROUP), 1)).astype(BF16)
    lower = iota2((GROUP, GROUP), 0) >= iota2((GROUP, GROUP), 1)
    sums = dot(parts, upper)
    across = sums[:8] + sums[8:16] + sums[16:24]
    downs = dot_nt(lower.astype(BF16), parts)
    down = downs[:, :8] + downs[:, 8:16] + downs[:, 16:24]
    column_out[0] = jnp.exp(down)
    for odd in range(2):
        for row in range(2):
            index = 2 * odd + row
            columns = pl.ds(odd * DK, DK)
            keys = key_ref[row, :, columns]
            within = jnp.where(
                lower,
                jnp.exp(jnp.minimum(down[:, index : index + 1] - across[index : index + 1, :], 0.0)),
                0.0,
            )
            masked_out[0, index] = within
            scores = (dot_nt(query_ref[row, :, columns], keys) * within).astype(BF16)
            product_out[0, index] = dot(
                scores, jnp.concatenate([keys, value_ref[row, :, columns]], axis=1)
            )


def solve_kernel(
    items, place_ref, ridge_ref, query_ref, key_ref, value_ref, within_ref, product_ref,
    column_ref, gram_ref, solution_out, partial_out,
):
    step = pl.program_id(0)
    pair = (place_ref[0] ^ (step // items)) * items + step % items
    lower = square_lower()
    diagonal = iota2((DK, DK), 0) == iota2((DK, DK), 1)
    tails = gram_ref[0, 0, pl.ds(2 * DK, TAIL), :].astype(F32)
    for row in range(2):
        folded = gram_ref[0, 0, pl.ds(row * DK, DK), :].astype(F32)
        turned = folded.T
        grams = (
            jnp.where(lower, folded, turned),
            jnp.where(diagonal, tails[row : row + 1], jnp.where(lower, turned, folded)),
        )
        for odd in range(2):
            index = 2 * odd + row
            columns = pl.ds(odd * DK, DK)
            gram = grams[odd].astype(BF16)
            ridge = ridge_ref[2 * pair + odd]
            keys = key_ref[row, :, columns]
            both = jnp.concatenate([keys, value_ref[row, :, columns]], axis=1)
            entering = column_ref[0, :, index : index + 1]
            queries = query_ref[row, :, columns]
            wide = queries.astype(F32)
            first = product_ref[0, index]
            applied = first[:, :DK] + entering * dot(queries, gram) + ridge * wide
            norm = jnp.sum(wide * wide, axis=-1, keepdims=True)
            size = norm / (jnp.sum(wide * applied, axis=-1, keepdims=True) + solve_epsilon)
            residual = wide - size * applied
            norm_next = jnp.sum(residual * residual, axis=-1, keepdims=True)
            direction = (residual + norm_next / (norm + solve_epsilon) * wide).astype(BF16)
            turn = direction.astype(F32)
            scores = (dot_nt(direction, keys) * within_ref[0, index]).astype(BF16)
            second = dot(scores, both)
            applied = second[:, :DK] + entering * dot(direction, gram) + ridge * turn
            size_next = norm_next / (
                jnp.sum(turn * applied, axis=-1, keepdims=True) + solve_epsilon
            )
            solution_out[row, :, columns] = (size * wide + size_next * turn).astype(BF16)
            partial_out[row, :, columns] = size * first[:, DK:] + size_next * second[:, DK:]


def readout_kernel(column_ref, gain_ref, solution_ref, partial_ref, memory_ref, normed_out):
    for row in range(2):
        for odd in range(2):
            index = 2 * odd + row
            columns = pl.ds(odd * DK, DK)
            memory = memory_ref[0, 0, pl.ds((2 * row + odd) * DK, DK), :]
            entering = column_ref[0, :, index : index + 1]
            readout = partial_ref[row, :, columns] + entering * dot(
                solution_ref[row, :, columns], memory
            )
            scale = lax.rsqrt(
                jnp.mean(readout * readout, axis=-1, keepdims=True) + norm_epsilon
            )
            normed_out[row, :, columns] = (readout * scale * gain_ref[:, columns]).astype(BF16)


def mix_kernel(parts, place_ref, *refs):
    left, right, out = refs[:parts], refs[parts : 2 * parts], refs[2 * parts]
    total = dot(left[0][...], right[0][...])
    for i in range(1, parts):
        total = total + dot(left[i][...], right[i][...])
    out[...] = total.astype(BF16)


def whole_blocks(count):
    return [pl.BlockSpec(memory_space=pltpu.VMEM)] * count


def params(limit_mib, dims=None):
    return pltpu.CompilerParams(vmem_limit_bytes=limit_mib * MIB, dimension_semantics=dims)


def on_device(queries, key_vectors, value_vectors, log_decay, ridge_shift, norm_gain, out_weight):
    block = queries.shape[1]
    heads = queries.shape[2] // DK
    pairs = heads // 2
    count = lax.axis_size("ctx")
    members = 1
    while pairs % (2 * members) == 0 and (2 * members) ** 2 <= count:
        members *= 2
    slabs = count // members
    steps = slabs.bit_length() - 1
    items = pairs // members
    mine = lax.axis_index("ctx")
    place = mine % members
    where = jnp.stack([place, mine // members]).astype(jnp.int32)
    smem = pl.BlockSpec(memory_space=pltpu.SMEM)

    def swap(value, distance):
        if distance == 0:
            return value
        return lax.ppermute(value, "ctx", [(i, i ^ distance) for i in range(count)])

    def run(kernel, shapes, *operands):
        return pl.pallas_call(
            kernel,
            out_shape=[jax.ShapeDtypeStruct(shape, BF16) for shape in shapes],
            in_specs=[smem] + whole_blocks(len(operands)),
            out_specs=whole_blocks(len(shapes)),
            compiler_params=params(16),
        )(where, *operands)

    gram_states, memory_states = pl.pallas_call(
        functools.partial(states_kernel, pairs),
        out_shape=[
            jax.ShapeDtypeStruct((pairs, ROWS_G, DK), BF16),
            jax.ShapeDtypeStruct((pairs, ROWS_M, DK), BF16),
        ],
        in_specs=whole_blocks(3),
        out_specs=whole_blocks(2),
        compiler_params=params(24),
    )(log_decay, key_vectors, value_vectors)

    def to_members(states, rows):
        pieces = states.reshape(members, items, rows, DK)
        return [
            swap(lax.dynamic_index_in_dim(pieces, place ^ d, 0, keepdims=False), d)
            for d in range(members)
        ]

    grams = to_members(gram_states, ROWS_G)
    memories = to_members(memory_states, ROWS_M)

    def shapes(kind, last):
        tail = TAIL if kind is Gram else 0
        one = (items, kind.rows + tail, DK)
        return [one, one] if last else [(items, 2 * kind.rows + tail, DK)]

    def first_message(kind, states):
        last = steps == 1
        return run(
            functools.partial(plane_kernel, kind, members, items, 0 if last else None),
            shapes(kind, last),
            *states,
            *grams,
        )

    messages_g = [first_message(Gram, grams)]
    messages_m = [first_message(Memory, memories)]
    got_g, got_m = [], []
    for step in range(steps):
        got_g.append(swap(messages_g[-1][0], members << step))
        got_m.append(swap(messages_m[-1][0], members << step))
        if step == steps - 1:
            break
        last = step == steps - 2
        bit_next = step + 1 if last else None
        own_g = messages_g[-1][0]
        for kind, messages, got in ((Gram, messages_g, got_g), (Memory, messages_m, got_m)):
            messages.append(
                run(
                    functools.partial(step_kernel, kind, items, step, bit_next),
                    shapes(kind, last),
                    messages[-1][0],
                    got[-1],
                    own_g,
                    got_g[-1],
                )
            )

    def replies(kind, states, got, keep, rows):
        backs = run(
            functools.partial(entering_kernel, kind, members, items, steps),
            [(items, rows, DK)] * members,
            *states,
            *grams,
            *got,
            *got_g,
            keep,
            messages_g[-1][0],
        )
        return jnp.stack([swap(back, d) for d, back in enumerate(backs)])

    entering_grams = replies(Gram, grams, got_g, messages_g[-1][1], ROWS_G)
    entering_memories = replies(Memory, memories, got_m, messages_m[-1][1], ROWS_M)

    lanes = pl.BlockSpec((2, block, PAIR), lambda i: (0, 0, i))
    square = (1, 4, GROUP, GROUP)
    within, product, column = pl.pallas_call(
        local_kernel,
        grid=(pairs,),
        out_shape=[
            jax.ShapeDtypeStruct((pairs,) + square[1:], F32),
            jax.ShapeDtypeStruct((pairs,) + square[1:], F32),
            jax.ShapeDtypeStruct((pairs, GROUP, 8), F32),
        ],
        in_specs=[pl.BlockSpec((2, 2, GROUP), lambda i: (i, 0, 0)), lanes, lanes, lanes],
        out_specs=[
            pl.BlockSpec(square, lambda i: (i, 0, 0, 0)),
            pl.BlockSpec(square, lambda i: (i, 0, 0, 0)),
            pl.BlockSpec((1, GROUP, 8), lambda i: (i, 0, 0)),
        ],
        compiler_params=params(24),
    )(log_decay, queries, key_vectors, value_vectors)

    def pair_at(i, where_ref):
        return (where_ref[0] ^ (i // items)) * items + i % items

    pair_lanes = pl.BlockSpec((2, block, PAIR), lambda i, w: (0, 0, pair_at(i, w)))
    pair_square = pl.BlockSpec(square, lambda i, w: (pair_at(i, w), 0, 0, 0))
    pair_column = pl.BlockSpec((1, GROUP, 8), lambda i, w: (pair_at(i, w), 0, 0))

    def state_block(rows):
        return pl.BlockSpec((1, 1, rows, DK), lambda i, w: (i // items, i % items, 0, 0))

    solution_rows, partial_rows = pl.pallas_call(
        functools.partial(solve_kernel, items),
        grid_spec=pltpu.PrefetchScalarGridSpec(
            num_scalar_prefetch=1,
            grid=(pairs,),
            in_specs=[
                smem, pair_lanes, pair_lanes, pair_lanes, pair_square, pair_square,
                pair_column, state_block(ROWS_G),
            ],
            out_specs=[pair_lanes, pair_lanes],
        ),
        out_shape=[
            jax.ShapeDtypeStruct(queries.shape, BF16),
            jax.ShapeDtypeStruct(queries.shape, F32),
        ],
        compiler_params=params(24),
    )(
        where, ridge_shift, queries, key_vectors, value_vectors, within, product, column,
        entering_grams,
    )
    normed = pl.pallas_call(
        lambda w, *refs: readout_kernel(*refs),
        grid_spec=pltpu.PrefetchScalarGridSpec(
            num_scalar_prefetch=1,
            grid=(pairs,),
            in_specs=[
                pair_column,
                pl.BlockSpec((1, PAIR), lambda i, w: (0, pair_at(i, w))),
                pair_lanes,
                pair_lanes,
                state_block(ROWS_M),
            ],
            out_specs=[pair_lanes],
        ),
        out_shape=[jax.ShapeDtypeStruct(queries.shape, BF16)],
        compiler_params=params(16),
    )(where, column, norm_gain.reshape(1, -1), solution_rows, partial_rows, entering_memories)[0]

    flattened = normed.reshape(2 * block, heads * DV)
    sides = lax.axis_size("head")
    side = lax.axis_index("head")
    lefts = [flattened] + [
        lax.ppermute(flattened, "head", [((i + d) % sides, i) for i in range(sides)])
        for d in range(1, sides)
    ]
    columns = out_weight.shape[1]
    width = min(columns, 512)
    mixed = pl.pallas_call(
        functools.partial(mix_kernel, sides),
        grid_spec=pltpu.PrefetchScalarGridSpec(
            num_scalar_prefetch=1,
            grid=(columns // width,),
            in_specs=[pl.BlockSpec(flattened.shape, lambda j, s: (0, 0))] * sides
            + [
                pl.BlockSpec(
                    (heads * DV, width), lambda j, s, d=d: (lax.rem(s[0] + d, sides), j)
                )
                for d in range(sides)
            ],
            out_specs=[pl.BlockSpec((2 * block, width), lambda j, s: (0, j))],
        ),
        out_shape=[jax.ShapeDtypeStruct((2 * block, columns), BF16)],
        compiler_params=params(40),
    )(side.reshape(1).astype(jnp.int32), *lefts, *([out_weight] * sides))[0]
    return mixed.reshape(2, block, columns)


def solution(mesh):
    return jax.shard_map(
        on_device,
        mesh=mesh,
        in_specs=(
            P(None, "ctx", "head"),
            P(None, "ctx", "head"),
            P(None, "ctx", "head"),
            P("head", None, "ctx"),
            P("head"),
            P("head"),
            P(None, "head"),
        ),
        out_specs=P(None, "ctx", "head"),
        check_vma=False,
    )
```

```python
import functools

import jax
import jax.numpy as jnp
from jax import lax
from jax.experimental import pallas as pl
from jax.experimental.pallas import tpu as pltpu
from jax.sharding import PartitionSpec as P

DK = 128
DV = 128
GROUP = 256
PAIR = 2 * DK
TAIL = 16
HALF = 3 * DK
ROWS = 2 * HALF + TAIL
ROWS_G = 2 * DK + TAIL
ROWS_M = 4 * DK
norm_epsilon = 1e-06
solve_epsilon = 1e-06

F32 = jnp.float32
BF16 = jnp.bfloat16
MIB = 1024 * 1024


def iota2(shape, dim):
    return lax.broadcasted_iota(jnp.int32, shape, dim)


def dot(a, b):
    return lax.dot_general(a, b, (((1,), (0,)), ((), ())), preferred_element_type=F32)


def dot_nt(a, b):
    return lax.dot_general(a, b, (((1,), (1,)), ((), ())), preferred_element_type=F32)


def split3(x):
    high = x.astype(BF16).astype(F32)
    middle = (x - high).astype(BF16).astype(F32)
    low = (x - high - middle).astype(BF16).astype(F32)
    return (high, middle, low)


def square_lower():
    return iota2((DK, DK), 0) >= iota2((DK, DK), 1)


def states_kernel(members, items, where_ref, rate_ref, key_hbm, value_hbm, *refs):
    outs, (keys_in, values_in) = refs[:members], refs[members : members + 2]
    weight_rows, log_tiles, key_sem, value_sem = refs[members + 2 :]
    pairs = members * items
    place = where_ref[0]

    def pair_of(d, item):
        return (place ^ d) * items + item

    def fetches(slot, pair):
        columns = pl.ds(pl.multiple_of(pair * PAIR, PAIR), PAIR)
        return (
            pltpu.make_async_copy(key_hbm.at[:, :, columns], keys_in.at[slot], key_sem.at[slot]),
            pltpu.make_async_copy(
                value_hbm.at[:, :, columns], values_in.at[slot], value_sem.at[slot]
            ),
        )

    for slot in range(pairs):
        for fetch in fetches(slot, pair_of(slot // items, slot % items)):
            fetch.start()
    rows = 4 * pairs
    rates = jnp.concatenate([rate_ref[h] for h in range(2 * pairs)], axis=0)
    parts = jnp.concatenate(split3(rates), axis=0).astype(BF16)
    upper = (iota2((GROUP, GROUP), 0) <= iota2((GROUP, GROUP), 1)).astype(BF16)
    sums = dot(parts, upper)
    cumulative = sums[:rows] + sums[rows : 2 * rows] + sums[2 * rows :]
    whole = dot(parts, jnp.ones((GROUP, DK), BF16))
    totals = whole[:rows] + whole[rows : 2 * rows] + whole[2 * rows :]
    weight_rows[...] = jnp.exp(
        jnp.minimum(jnp.concatenate([totals, totals], axis=1) - cumulative, 0.0)
    )
    for third, part in enumerate(split3(totals)):
        log_tiles[third] = part
    lower = square_lower()
    diagonal = iota2((DK, DK), 0) == iota2((DK, DK), 1)
    for slot in range(pairs):
        d, item = slot // items, slot % items
        pair = pair_of(d, item)
        for fetch in fetches(slot, pair):
            fetch.wait()
        tail = []
        for row in range(2):
            grams = []
            for odd in range(2):
                index = 4 * pair + 2 * odd + row
                keys = keys_in[slot, row, :, odd * DK : (odd + 1) * DK]
                values = values_in[slot, row, :, odd * DK : (odd + 1) * DK]
                turned = keys.astype(F32).T * weight_rows[pl.ds(index, 1), :]
                product = dot(turned.astype(BF16), jnp.concatenate([keys, values], axis=1))
                grams.append(product[:, :DK])
                start = row * HALF + (1 + odd) * DK
                outs[d][item, pl.ds(start, DK), :] = product[:, DK:].astype(BF16)
            folded = jnp.where(lower, grams[0], grams[1])
            outs[d][item, pl.ds(row * HALF, DK), :] = folded.astype(BF16)
            tail.append(jnp.sum(jnp.where(diagonal, grams[1], 0.0), axis=0, keepdims=True))
        for row in range(2):
            for odd in range(2):
                index = 4 * pair + 2 * odd + row
                tail += [log_tiles[third, pl.ds(index, 1), :] for third in range(3)]
        tail.append(jnp.zeros((2, DK), F32))
        outs[d][item, pl.ds(2 * HALF, TAIL), :] = jnp.concatenate(tail, axis=0).astype(BF16)


def read_tail(block):
    def one(start):
        return block[start : start + 1] + block[start + 1 : start + 2] + block[start + 2 : start + 3]

    logs = {("F", 0): one(2), ("F", 1): one(5), ("B", 0): one(8), ("B", 1): one(11)}
    return (block[0:1], block[1:2]), logs


def read_state(load, start, diagonal, parts):
    state = {}
    if "gram" in parts:
        state["gram"] = load(start, DK)
        state["diagonal"] = diagonal
    if "memory" in parts:
        state["even"] = load(start + DK, DK)
        state["odd"] = load(start + 2 * DK, DK)
    return state


def loader(ref, *lead):
    return lambda start, rows: ref[(*lead, pl.ds(start, rows), slice(None))].astype(F32)


def read_message(load, count, parts):
    diagonals, logs = read_tail(load(count * HALF, TAIL))
    states = [read_state(load, i * HALF, diagonals[i], parts) for i in range(count)]
    return states, logs


def scaled(state, weights):
    out = {}
    for name, value in state.items():
        if name == "gram":
            out[name] = value * jnp.where(square_lower(), weights[0], weights[1])
        else:
            out[name] = value * weights[0 if name == "even" else 1]
    return out


def plus(a, b):
    return {name: a[name] + b[name] for name in a}


def pick(flag, a, b):
    return jnp.where(flag, a, b)


def exps(logs, name):
    return [jnp.exp(logs[name, odd]) for odd in range(2)]


def write_tail(diagonals, logs):
    rows = list(diagonals) + [jnp.zeros((1, DK), F32)] * (2 - len(diagonals))
    for key in (("F", 0), ("F", 1), ("B", 0), ("B", 1)):
        rows += split3(logs[key]) if logs is not None else [jnp.zeros((3, DK), F32)]
    rows.append(jnp.zeros((2, DK), F32))
    return jnp.concatenate(rows, axis=0).astype(BF16)


def write_message(ref, item, states, logs):
    for i, state in enumerate(states):
        for j, name in enumerate(("gram", "even", "odd")):
            ref[item, pl.ds(i * HALF + j * DK, DK), :] = state[name].astype(BF16)
    ref[item, pl.ds(len(states) * HALF, TAIL), :] = write_tail(
        [state["diagonal"] for state in states], logs
    )


BOTH = ("gram", "memory")


def emit(item, front, back, logs, last_bit, outs):
    if last_bit is None:
        write_message(outs[0], item, [front, back], logs)
        return
    upper = last_bit == 1
    weights = [pick(upper, w, 1.0) for w in exps(logs, "B")]
    kept = {name: pick(upper, value, 0.0) for name, value in back.items()}
    write_message(outs[0], item, [plus(scaled(front, weights), kept)], logs)
    write_message(outs[1], item, [front], logs)


def gather_members(members, state_refs, stacked):
    for d in range(members):
        stacked[d] = state_refs[d][...]


def plane_kernel(members, items, bit_next, where_ref, *refs):
    state_refs, outs, stacked = refs[:members], refs[members + 1 : -1], refs[-1]
    gather_members(members, state_refs, stacked)
    last_bit = None if bit_next is None else (where_ref[1] >> bit_next) & 1
    for item in range(items):
        front = back = None
        total = None
        for member in range(members):
            (state, _), logs = read_message(
                loader(stacked, where_ref[0] ^ member, item), 2, BOTH
            )
            front = state if front is None else plus(scaled(front, exps(logs, "F")), state)
            total = logs if total is None else {key: total[key] + logs[key] for key in logs}
        for member in reversed(range(members)):
            (_, state), logs = read_message(
                loader(stacked, where_ref[0] ^ member, item), 2, BOTH
            )
            back = state if back is None else plus(scaled(back, exps(logs, "B")), state)
        emit(item, front, back, total, last_bit, outs)


def step_kernel(items, bit, bit_next, where_ref, own_ref, got_ref, *outs):
    upper = ((where_ref[1] >> bit) & 1) == 1
    last_bit = None if bit_next is None else (where_ref[1] >> bit_next) & 1
    for item in range(items):
        own, mine = read_message(loader(own_ref, item), 2, BOTH)
        got, theirs = read_message(loader(got_ref, item), 2, BOTH)
        sides = []
        for which, name in enumerate(("F", "B")):
            own_first = upper if name == "B" else jnp.logical_not(upper)
            own_weights = [pick(own_first, w, 1.0) for w in exps(theirs, name)]
            got_weights = [pick(own_first, 1.0, w) for w in exps(mine, name)]
            sides.append(plus(scaled(own[which], own_weights), scaled(got[which], got_weights)))
        total = {key: mine[key] + theirs[key] for key in mine}
        emit(item, sides[0], sides[1], total, last_bit, outs)


def entering_kernel(parts, members, items, steps, where_ref, *refs):
    state_refs, got_refs = refs[:members], refs[members : members + steps]
    keep_ref, outs = refs[members + steps], refs[members + steps + 2 : -2]
    stacked, ready = refs[-2:]
    gather_members(members, state_refs, stacked)
    gram, memory = "gram" in parts, "memory" in parts

    def place(member, item, which, state):
        slot = where_ref[0] ^ member
        if gram:
            ready[slot, item, pl.ds(which * DK, DK), :] = state["gram"].astype(BF16)
        if memory:
            for odd, name in enumerate(("even", "odd")):
                start = (2 * which + odd) * DK
                ready[slot, item, pl.ds(start, DK), :] = state[name].astype(BF16)

    for item in range(items):
        zero = jnp.zeros((1, DK), F32)
        late = {key: zero for key in (("F", 0), ("F", 1), ("B", 0), ("B", 1))}
        front = back = None
        for step in range(steps):
            upper = ((where_ref[1] >> step) & 1) == 1
            last = step == steps - 1
            got, theirs = read_message(loader(got_refs[step], item), 1 if last else 2, parts)
            add = scaled(got[0], [pick(upper, w, 0.0) for w in exps(late, "F")])
            front = add if front is None else plus(front, add)
            if not last:
                add = scaled(got[1], [pick(upper, 0.0, w) for w in exps(late, "B")])
                for odd in range(2):
                    late["F", odd] = late["F", odd] + pick(upper, theirs["F", odd], 0.0)
                    late["B", odd] = late["B", odd] + pick(upper, 0.0, theirs["B", odd])
            else:
                (kept,), mine = read_message(loader(keep_ref, item), 1, parts)
                keep_weights, got_weights = [], []
                for odd in range(2):
                    through = theirs["F", odd] + theirs["B", odd]
                    keep_weights.append(jnp.exp(late["B", odd] + pick(upper, 0.0, through)))
                    got_weights.append(jnp.exp(late["B", odd] + pick(upper, mine["F", odd], 0.0)))
                add = plus(scaled(kept, keep_weights), scaled(got[0], got_weights))
            back = add if back is None else plus(back, add)
        tails = [[None] * 2 for _ in range(members)]
        for member in range(members):
            place(member, item, 0, front)
            tails[member][0] = front.get("diagonal", zero)
            if member < members - 1:
                (state, _), logs = read_message(
                    loader(stacked, where_ref[0] ^ member, item), 2, parts
                )
                front = plus(scaled(front, exps(logs, "F")), state)
        for member in reversed(range(members)):
            place(member, item, 1, back)
            tails[member][1] = back.get("diagonal", zero)
            if member > 0:
                (_, state), logs = read_message(
                    loader(stacked, where_ref[0] ^ member, item), 2, parts
                )
                back = plus(scaled(back, exps(logs, "B")), state)
        if gram:
            for member in range(members):
                slot = where_ref[0] ^ member
                ready[slot, item, pl.ds(2 * DK, TAIL), :] = write_tail(tails[member], None)
    for d in range(members):
        outs[d][...] = ready[d]


def local_kernel(
    items, pairs, where_ref, rate_ref, query_hbm, key_ref, value_ref, weight_hbm,
    masked_out, product_out, column_out, weight_out, query_out, weight_sem, query_sem,
):
    def pair_of(slot):
        return (where_ref[0] ^ (slot // items)) * items + slot % items

    fetches = []
    for slot in range(pairs):
        columns = pl.ds(pl.multiple_of(pair_of(slot) * PAIR, PAIR), PAIR)
        fetches.append(
            pltpu.make_async_copy(
                query_hbm.at[:, :, columns], query_out.at[slot], query_sem.at[slot]
            )
        )
        fetches[-1].start()
    weight_fetch = pltpu.make_async_copy(weight_hbm, weight_out, weight_sem)
    weight_fetch.start()
    upper = (iota2((GROUP, GROUP), 0) <= iota2((GROUP, GROUP), 1)).astype(BF16)
    lower = iota2((GROUP, GROUP), 0) >= iota2((GROUP, GROUP), 1)
    lower_ones = lower.astype(BF16)
    for fetch in fetches:
        fetch.wait()

    @pl.loop(0, pairs)
    def _(slot):
        pair = pair_of(slot)
        rates = jnp.concatenate([rate_ref[2 * pair + odd] for odd in range(2)], axis=0)
        rates = jnp.concatenate([rates, jnp.zeros((4, GROUP), F32)], axis=0)
        parts = jnp.concatenate(split3(rates) + (jnp.zeros((8, GROUP), F32),), axis=0).astype(BF16)
        sums = dot(parts, upper)
        across = sums[:8] + sums[8:16] + sums[16:24]
        downs = dot_nt(lower_ones, parts)
        down = downs[:, :8] + downs[:, 8:16] + downs[:, 16:24]
        fading = jnp.exp(down)
        raw = {}
        for odd in range(2):
            for row in range(2):
                index = 2 * odd + row
                column_out[slot, index] = jnp.broadcast_to(
                    fading[:, index : index + 1], (GROUP, DK)
                )
                columns = slice(odd * DK, (odd + 1) * DK)
                raw[index] = dot_nt(query_out[slot, row, :, columns], key_ref[slot, row, :, columns])
        scores = {}
        for index in range(4):
            within = jnp.where(
                lower,
                jnp.exp(
                    jnp.minimum(down[:, index : index + 1] - across[index : index + 1, :], 0.0)
                ),
                0.0,
            )
            masked_out[slot, index] = within
            scores[index] = (raw[index] * within).astype(BF16)
        for odd in range(2):
            for row in range(2):
                index = 2 * odd + row
                columns = slice(odd * DK, (odd + 1) * DK)
                both = jnp.concatenate(
                    [key_ref[slot, row, :, columns], value_ref[slot, row, :, columns]], axis=1
                )
                product_out[slot, index] = dot(scores[index], both)

    weight_fetch.wait()


def sum_lanes(x):
    high = x.astype(BF16)
    low = (x - high.astype(F32)).astype(BF16)
    return dot(jnp.concatenate([high, low], axis=1), jnp.ones((2 * x.shape[1], DK), BF16))


def solve_kernel(
    items, pairs, where_ref, ridge_ref, query_ref, key_ref, value_ref, within_ref, product_ref,
    column_ref, gram_ref, weight_ref, solution_out, partial_out,
):
    lower = square_lower()
    diagonal = iota2((DK, DK), 0) == iota2((DK, DK), 1)
    cases = [(row, odd) for row in range(2) for odd in range(2)]
    lanes = [slice(odd * DK, (odd + 1) * DK) for odd in range(2)]

    @pl.loop(0, pairs)
    def _(slot):
        d, item = slot // items, slot % items
        pair = (where_ref[0] ^ d) * items + item
        tails = gram_ref[d, item, pl.ds(2 * DK, TAIL), :].astype(F32)
        grams = {}
        for row in range(2):
            folded = gram_ref[d, item, pl.ds(row * DK, DK), :].astype(F32)
            turned = folded.T
            grams[row, 0] = jnp.where(lower, folded, turned).astype(BF16)
            grams[row, 1] = jnp.where(
                diagonal, tails[row : row + 1], jnp.where(lower, turned, folded)
            ).astype(BF16)

        def entering(row, odd):
            return column_ref[slot, 2 * odd + row]

        def wide(row, odd):
            return query_ref[slot, row, :, lanes[odd]].astype(F32)

        carried = {(r, o): dot(query_ref[slot, r, :, lanes[o]], grams[r, o]) for r, o in cases}
        norm = {(r, o): sum_lanes(wide(r, o) * wide(r, o)) for r, o in cases}
        applied = {
            (r, o): product_ref[slot, 2 * o + r, :, :DK]
            + entering(r, o) * carried[r, o]
            + ridge_ref[2 * pair + o] * wide(r, o)
            for r, o in cases
        }
        curve = {(r, o): sum_lanes(wide(r, o) * applied[r, o]) for r, o in cases}
        size = {case: norm[case] / (curve[case] + solve_epsilon) for case in cases}
        residual = {case: wide(*case) - size[case] * applied[case] for case in cases}
        norm_next = {case: sum_lanes(residual[case] * residual[case]) for case in cases}
        direction = {
            case: (
                residual[case] + norm_next[case] / (norm[case] + solve_epsilon) * wide(*case)
            ).astype(BF16)
            for case in cases
        }
        raw = {(r, o): dot_nt(direction[r, o], key_ref[slot, r, :, lanes[o]]) for r, o in cases}
        carried = {case: dot(direction[case], grams[case]) for case in cases}
        scores = {
            (r, o): (raw[r, o] * within_ref[slot, 2 * o + r]).astype(BF16) for r, o in cases
        }
        second = {
            (r, o): dot(
                scores[r, o],
                jnp.concatenate(
                    [key_ref[slot, r, :, lanes[o]], value_ref[slot, r, :, lanes[o]]], axis=1
                ),
            )
            for r, o in cases
        }
        turn = {case: direction[case].astype(F32) for case in cases}
        applied = {
            (r, o): second[r, o][:, :DK]
            + entering(r, o) * carried[r, o]
            + ridge_ref[2 * pair + o] * turn[r, o]
            for r, o in cases
        }
        curve = {case: sum_lanes(turn[case] * applied[case]) for case in cases}
        for r, o in cases:
            size_next = norm_next[r, o] / (curve[r, o] + solve_epsilon)
            solution_out[slot, r, :, lanes[o]] = (
                size[r, o] * wide(r, o) + size_next * turn[r, o]
            ).astype(BF16)
            partial_out[slot, r, :, lanes[o]] = (
                size[r, o] * product_ref[slot, 2 * o + r, :, DK:]
                + size_next * second[r, o][:, DK:]
            )


def readout_kernel(
    items, pairs, where_ref, column_ref, gain_ref, solution_ref, partial_ref, memory_ref,
    weight_ref, normed_out,
):
    cases = [(row, odd) for row in range(2) for odd in range(2)]
    lanes = [slice(odd * DK, (odd + 1) * DK) for odd in range(2)]
    for slot in range(pairs):
        d, item = slot // items, slot % items
        pair = (where_ref[0] ^ d) * items + item
        readout = {
            (r, o): partial_ref[slot, r, :, lanes[o]]
            + column_ref[slot, 2 * o + r]
            * dot(
                solution_ref[slot, r, :, lanes[o]],
                memory_ref[d, item, pl.ds((2 * r + o) * DK, DK), :],
            )
            for r, o in cases
        }
        square = {case: sum_lanes(readout[case] * readout[case]) for case in cases}
        for r, o in cases:
            columns = pl.ds(pl.multiple_of(pair * PAIR + o * DK, DK), DK)
            scale = lax.rsqrt(square[r, o] * (1.0 / DV) + norm_epsilon)
            normed_out[r, :, columns] = (readout[r, o] * scale * gain_ref[:, columns]).astype(BF16)


def own_mix_kernel(tiles, side_ref, left_ref, weight_ref, out_ref):
    depth, width = left_ref.shape[1], out_ref.shape[1] // tiles
    rows = pl.ds(pl.multiple_of(side_ref[0] * depth, depth), depth)

    @pl.loop(0, tiles)
    def _(tile):
        columns = pl.ds(pl.multiple_of(tile * width, width), width)
        out_ref[:, columns] = dot(left_ref[...], weight_ref[rows, columns])


def last_mix_kernel(others, sides, side_ref, own_ref, weight_ref, *refs):
    lefts, out_ref = refs[:others], refs[others]
    depth, width = lefts[0].shape[1], out_ref.shape[1]
    columns = pl.ds(pl.multiple_of(pl.program_id(0) * width, width), width)
    total = own_ref[:, columns]
    for i, left in enumerate(lefts):
        source = lax.rem(side_ref[0] + i + 1, sides)
        rows = pl.ds(pl.multiple_of(source * depth, depth), depth)
        total = total + dot(left[...], weight_ref[rows, columns])
    out_ref[...] = total.astype(BF16)


def whole_blocks(count):
    return [pl.BlockSpec(memory_space=pltpu.VMEM)] * count


def cost(mflops, kib):
    return pl.CostEstimate(
        flops=mflops * 1_000_000, bytes_accessed=kib * 1024, transcendentals=0
    )


def params(limit_mib, dims=None):
    return pltpu.CompilerParams(vmem_limit_bytes=limit_mib * MIB, dimension_semantics=dims)


def on_device(queries, key_vectors, value_vectors, log_decay, ridge_shift, norm_gain, out_weight):
    block = queries.shape[1]
    heads = queries.shape[2] // DK
    pairs = heads // 2
    count = lax.axis_size("ctx")
    members = 1
    while pairs % (2 * members) == 0 and (2 * members) ** 2 <= count:
        members *= 2
    slabs = count // members
    steps = slabs.bit_length() - 1
    items = pairs // members
    mine = lax.axis_index("ctx")
    place = mine % members
    where = jnp.stack([place, mine // members]).astype(jnp.int32)
    smem = pl.BlockSpec(memory_space=pltpu.SMEM)

    def swap(value, distance):
        if distance == 0:
            return value
        return lax.ppermute(value, "ctx", [(i, i ^ distance) for i in range(count)])

    def run(kernel, shapes, scratch, *operands):
        return pl.pallas_call(
            kernel,
            out_shape=[jax.ShapeDtypeStruct(shape, BF16) for shape in shapes],
            in_specs=[smem] + whole_blocks(len(operands)),
            out_specs=whole_blocks(len(shapes)),
            scratch_shapes=[pltpu.VMEM(shape, BF16) for shape in scratch],
            compiler_params=params(12),
        )(where, *operands)

    def in_hbm(*values):
        return [pltpu.with_memory_space_constraint(value, pltpu.HBM) for value in values]

    message = (items, ROWS, DK)
    hbm = pl.BlockSpec(memory_space=pltpu.HBM)
    rows_by_slot = jax.ShapeDtypeStruct((pairs, 2, block, PAIR), BF16)
    *states, keys, values = pl.pallas_call(
        functools.partial(states_kernel, members, items),
        out_shape=[jax.ShapeDtypeStruct(message, BF16)] * members + [rows_by_slot] * 2,
        in_specs=[smem] + whole_blocks(1) + [hbm, hbm],
        out_specs=whole_blocks(members + 2),
        scratch_shapes=[
            pltpu.VMEM((4 * pairs, GROUP), F32),
            pltpu.VMEM((3, 4 * pairs, DK), F32),
            pltpu.SemaphoreType.DMA((pairs,)),
            pltpu.SemaphoreType.DMA((pairs,)),
        ],
        compiler_params=params(16),
        cost_estimate=cost(0, 0),
    )(where, log_decay, *in_hbm(key_vectors, value_vectors))
    slab = [swap(state, d) for d, state in enumerate(states)]

    square = (pairs, 4, GROUP, GROUP)
    within, product, column, weight, query_rows = pl.pallas_call(
        functools.partial(local_kernel, items, pairs),
        out_shape=[
            jax.ShapeDtypeStruct(square, F32),
            jax.ShapeDtypeStruct(square, F32),
            jax.ShapeDtypeStruct((pairs, 4, GROUP, DK), F32),
            jax.ShapeDtypeStruct(out_weight.shape, BF16),
            rows_by_slot,
        ],
        in_specs=[smem] + whole_blocks(1) + [hbm] + whole_blocks(2) + [hbm],
        out_specs=whole_blocks(5),
        scratch_shapes=[pltpu.SemaphoreType.DMA(()), pltpu.SemaphoreType.DMA((pairs,))],
        compiler_params=params(16),
        cost_estimate=cost(4000, 4000),
    )(where, log_decay, *in_hbm(queries), keys, values, *in_hbm(out_weight))

    def shapes(last):
        return [(items, HALF + TAIL, DK)] * 2 if last else [message]

    bit_next = 0 if steps == 1 else None
    messages = run(
        functools.partial(plane_kernel, members, items, bit_next),
        shapes(steps == 1),
        [(members,) + message],
        *slab,
        weight,
    )
    got = []
    for step in range(steps):
        got.append(swap(messages[0], members << step))
        if step == steps - 1:
            break
        last = step == steps - 2
        messages = run(
            functools.partial(step_kernel, items, step, step + 1 if last else None),
            shapes(last),
            [],
            messages[0],
            got[-1],
        )

    def replies(part, rows, after):
        backs = run(
            functools.partial(entering_kernel, (part,), members, items, steps),
            [(items, rows, DK)] * members,
            [(members,) + message, (members, items, rows, DK)],
            *slab,
            *got,
            messages[1],
            after,
        )
        return jnp.stack([swap(back, d) for d, back in enumerate(backs)]), backs[0]

    entering_grams, after = replies("gram", ROWS_G, weight)
    entering_memories, _ = replies("memory", ROWS_M, after)

    solution_rows, partial_rows = pl.pallas_call(
        functools.partial(solve_kernel, items, pairs),
        in_specs=[smem, smem] + whole_blocks(8),
        out_specs=whole_blocks(2),
        out_shape=[rows_by_slot, jax.ShapeDtypeStruct(rows_by_slot.shape, F32)],
        compiler_params=params(12),
        cost_estimate=cost(4000, 4000),
    )(
        where, ridge_shift, query_rows, keys, values, within, product, column, entering_grams,
        weight,
    )
    normed = pl.pallas_call(
        functools.partial(readout_kernel, items, pairs),
        in_specs=[smem] + whole_blocks(6),
        out_specs=whole_blocks(1)[0],
        out_shape=jax.ShapeDtypeStruct(queries.shape, BF16),
        compiler_params=params(16),
    )(
        where, column, norm_gain.reshape(1, -1), solution_rows, partial_rows, entering_memories,
        weight,
    )

    flattened = normed.reshape(2 * block, heads * DV)
    sides = lax.axis_size("head")
    side = lax.axis_index("head").reshape(1).astype(jnp.int32)
    lefts = [
        lax.ppermute(flattened, "head", [((i + d) % sides, i) for i in range(sides)])
        for d in range(1, sides)
    ]
    columns = out_weight.shape[1]
    width = min(columns, 512)
    own = pl.pallas_call(
        functools.partial(own_mix_kernel, columns // width),
        in_specs=[smem] + whole_blocks(2),
        out_specs=whole_blocks(1)[0],
        out_shape=jax.ShapeDtypeStruct((2 * block, columns), F32),
        compiler_params=params(12),
        cost_estimate=cost(2000, 2000),
    )(side, flattened, weight)
    mixed = pl.pallas_call(
        functools.partial(last_mix_kernel, sides - 1, sides),
        grid=(columns // width,),
        in_specs=[smem] + whole_blocks(1 + sides),
        out_specs=pl.BlockSpec((2 * block, width), lambda j: (0, j)),
        out_shape=jax.ShapeDtypeStruct((2 * block, columns), BF16),
        compiler_params=params(12),
    )(side, own, weight, *lefts)
    return mixed.reshape(2, block, columns)


def solution(mesh):
    return jax.shard_map(
        on_device,
        mesh=mesh,
        in_specs=(
            P(None, "ctx", "head"),
            P(None, "ctx", "head"),
            P(None, "ctx", "head"),
            P("head", None, "ctx"),
            P("head"),
            P("head"),
            P(None, "head"),
        ),
        out_specs=P(None, "ctx", "head"),
        check_vma=False,
    )
```

```python
import functools

import jax
import jax.numpy as jnp
from jax import lax
from jax.experimental import pallas as pl
from jax.experimental.pallas import tpu as pltpu
from jax.sharding import PartitionSpec as P

DK = 128
DV = 128
GROUP = 256
PAIR = 2 * DK
TAIL = 16
HALF = 3 * DK
ROWS = 2 * HALF + TAIL
ROWS_G = 2 * DK + TAIL
ROWS_M = 4 * DK
norm_epsilon = 1e-06
solve_epsilon = 1e-06

F32 = jnp.float32
BF16 = jnp.bfloat16
MIB = 1024 * 1024


def iota2(shape, dim):
    return lax.broadcasted_iota(jnp.int32, shape, dim)


def dot(a, b):
    return lax.dot_general(a, b, (((1,), (0,)), ((), ())), preferred_element_type=F32)


def dot_nt(a, b):
    return lax.dot_general(a, b, (((1,), (1,)), ((), ())), preferred_element_type=F32)


def split3(x):
    high = x.astype(BF16).astype(F32)
    middle = (x - high).astype(BF16).astype(F32)
    low = (x - high - middle).astype(BF16).astype(F32)
    return (high, middle, low)


def square_lower():
    return iota2((DK, DK), 0) >= iota2((DK, DK), 1)


def states_kernel(members, items, where_ref, rate_hbm, key_hbm, value_hbm, *refs):
    outs, (keys_in, values_in, rate_ref) = refs[:members], refs[members : members + 3]
    weight_rows, log_tiles, key_sem, value_sem, rate_sem = refs[members + 3 :]
    rate_fetch = pltpu.make_async_copy(rate_hbm, rate_ref, rate_sem)
    rate_fetch.start()
    pairs = members * items
    place = where_ref[0]

    def pair_of(d, item):
        return (place ^ d) * items + item

    def fetches(slot, pair):
        columns = pl.ds(pl.multiple_of(pair * PAIR, PAIR), PAIR)
        return (
            pltpu.make_async_copy(key_hbm.at[:, :, columns], keys_in.at[slot], key_sem.at[slot]),
            pltpu.make_async_copy(
                value_hbm.at[:, :, columns], values_in.at[slot], value_sem.at[slot]
            ),
        )

    for slot in range(pairs):
        for fetch in fetches(slot, pair_of(slot // items, slot % items)):
            fetch.start()
    rate_fetch.wait()
    rows = 4 * pairs
    rates = jnp.concatenate([rate_ref[h] for h in range(2 * pairs)], axis=0)
    parts = jnp.concatenate(split3(rates), axis=0).astype(BF16)
    upper = (iota2((GROUP, GROUP), 0) <= iota2((GROUP, GROUP), 1)).astype(BF16)
    sums = dot(parts, upper)
    cumulative = sums[:rows] + sums[rows : 2 * rows] + sums[2 * rows :]
    whole = dot(parts, jnp.ones((GROUP, DK), BF16))
    totals = whole[:rows] + whole[rows : 2 * rows] + whole[2 * rows :]
    weight_rows[...] = jnp.exp(
        jnp.minimum(jnp.concatenate([totals, totals], axis=1) - cumulative, 0.0)
    )
    for third, part in enumerate(split3(totals)):
        log_tiles[third] = part
    lower = square_lower()
    diagonal = iota2((DK, DK), 0) == iota2((DK, DK), 1)
    for slot in range(pairs):
        d, item = slot // items, slot % items
        pair = pair_of(d, item)
        for fetch in fetches(slot, pair):
            fetch.wait()
        tail = []
        for row in range(2):
            grams = []
            for odd in range(2):
                index = 4 * pair + 2 * odd + row
                keys = keys_in[slot, row, :, odd * DK : (odd + 1) * DK]
                values = values_in[slot, row, :, odd * DK : (odd + 1) * DK]
                turned = keys.astype(F32).T * weight_rows[pl.ds(index, 1), :]
                product = dot(turned.astype(BF16), jnp.concatenate([keys, values], axis=1))
                grams.append(product[:, :DK])
                start = row * HALF + (1 + odd) * DK
                outs[d][item, pl.ds(start, DK), :] = product[:, DK:].astype(BF16)
            folded = jnp.where(lower, grams[0], grams[1])
            outs[d][item, pl.ds(row * HALF, DK), :] = folded.astype(BF16)
            tail.append(jnp.sum(jnp.where(diagonal, grams[1], 0.0), axis=0, keepdims=True))
        for row in range(2):
            for odd in range(2):
                index = 4 * pair + 2 * odd + row
                tail += [log_tiles[third, pl.ds(index, 1), :] for third in range(3)]
        tail.append(jnp.zeros((2, DK), F32))
        outs[d][item, pl.ds(2 * HALF, TAIL), :] = jnp.concatenate(tail, axis=0).astype(BF16)


def read_tail(block):
    def one(start):
        return block[start : start + 1] + block[start + 1 : start + 2] + block[start + 2 : start + 3]

    logs = {("F", 0): one(2), ("F", 1): one(5), ("B", 0): one(8), ("B", 1): one(11)}
    return (block[0:1], block[1:2]), logs


def read_state(load, start, diagonal, parts):
    state = {}
    if "gram" in parts:
        state["gram"] = load(start, DK)
        state["diagonal"] = diagonal
    if "memory" in parts:
        state["even"] = load(start + DK, DK)
        state["odd"] = load(start + 2 * DK, DK)
    return state


def loader(ref, *lead):
    return lambda start, rows: ref[(*lead, pl.ds(start, rows), slice(None))].astype(F32)


def read_message(load, count, parts):
    diagonals, logs = read_tail(load(count * HALF, TAIL))
    states = [read_state(load, i * HALF, diagonals[i], parts) for i in range(count)]
    return states, logs


def scaled(state, weights):
    out = {}
    for name, value in state.items():
        if name == "gram":
            out[name] = value * jnp.where(square_lower(), weights[0], weights[1])
        else:
            out[name] = value * weights[0 if name == "even" else 1]
    return out


def plus(a, b):
    return {name: a[name] + b[name] for name in a}


def pick(flag, a, b):
    return jnp.where(flag, a, b)


def exps(logs, name):
    return [jnp.exp(logs[name, odd]) for odd in range(2)]


def write_tail(diagonals, logs):
    rows = list(diagonals) + [jnp.zeros((1, DK), F32)] * (2 - len(diagonals))
    for key in (("F", 0), ("F", 1), ("B", 0), ("B", 1)):
        rows += split3(logs[key]) if logs is not None else [jnp.zeros((3, DK), F32)]
    rows.append(jnp.zeros((2, DK), F32))
    return jnp.concatenate(rows, axis=0).astype(BF16)


def write_message(ref, item, states, logs):
    for i, state in enumerate(states):
        for j, name in enumerate(("gram", "even", "odd")):
            ref[item, pl.ds(i * HALF + j * DK, DK), :] = state[name].astype(BF16)
    ref[item, pl.ds(len(states) * HALF, TAIL), :] = write_tail(
        [state["diagonal"] for state in states], logs
    )


BOTH = ("gram", "memory")


def emit(item, front, back, logs, last_bit, outs):
    if last_bit is None:
        write_message(outs[0], item, [front, back], logs)
        return
    upper = last_bit == 1
    weights = [pick(upper, w, 1.0) for w in exps(logs, "B")]
    kept = {name: pick(upper, value, 0.0) for name, value in back.items()}
    write_message(outs[0], item, [plus(scaled(front, weights), kept)], logs)
    write_message(outs[1], item, [front], logs)


def gather_members(members, state_refs, stacked):
    for d in range(members):
        stacked[d] = state_refs[d][...]


def plane_kernel(members, items, bit_next, where_ref, *refs):
    state_refs, outs, stacked = refs[:members], refs[members + 1 : -1], refs[-1]
    gather_members(members, state_refs, stacked)
    last_bit = None if bit_next is None else (where_ref[1] >> bit_next) & 1
    for item in range(items):
        front = back = None
        total = None
        for member in range(members):
            (state, _), logs = read_message(
                loader(stacked, where_ref[0] ^ member, item), 2, BOTH
            )
            front = state if front is None else plus(scaled(front, exps(logs, "F")), state)
            total = logs if total is None else {key: total[key] + logs[key] for key in logs}
        for member in reversed(range(members)):
            (_, state), logs = read_message(
                loader(stacked, where_ref[0] ^ member, item), 2, BOTH
            )
            back = state if back is None else plus(scaled(back, exps(logs, "B")), state)
        emit(item, front, back, total, last_bit, outs)


def step_kernel(items, bit, bit_next, where_ref, own_ref, got_ref, *outs):
    upper = ((where_ref[1] >> bit) & 1) == 1
    last_bit = None if bit_next is None else (where_ref[1] >> bit_next) & 1
    for item in range(items):
        own, mine = read_message(loader(own_ref, item), 2, BOTH)
        got, theirs = read_message(loader(got_ref, item), 2, BOTH)
        sides = []
        for which, name in enumerate(("F", "B")):
            own_first = upper if name == "B" else jnp.logical_not(upper)
            own_weights = [pick(own_first, w, 1.0) for w in exps(theirs, name)]
            got_weights = [pick(own_first, 1.0, w) for w in exps(mine, name)]
            sides.append(plus(scaled(own[which], own_weights), scaled(got[which], got_weights)))
        total = {key: mine[key] + theirs[key] for key in mine}
        emit(item, sides[0], sides[1], total, last_bit, outs)


def entering_kernel(parts, members, items, steps, where_ref, *refs):
    state_refs, got_refs = refs[:members], refs[members : members + steps]
    keep_ref, outs = refs[members + steps], refs[members + steps + 2 : -2]
    stacked, ready = refs[-2:]
    gather_members(members, state_refs, stacked)
    gram, memory = "gram" in parts, "memory" in parts

    def place(member, item, which, state):
        slot = where_ref[0] ^ member
        if gram:
            ready[slot, item, pl.ds(which * DK, DK), :] = state["gram"].astype(BF16)
        if memory:
            for odd, name in enumerate(("even", "odd")):
                start = (2 * which + odd) * DK
                ready[slot, item, pl.ds(start, DK), :] = state[name].astype(BF16)

    for item in range(items):
        zero = jnp.zeros((1, DK), F32)
        late = {key: zero for key in (("F", 0), ("F", 1), ("B", 0), ("B", 1))}
        front = back = None
        for step in range(steps):
            upper = ((where_ref[1] >> step) & 1) == 1
            last = step == steps - 1
            got, theirs = read_message(loader(got_refs[step], item), 1 if last else 2, parts)
            add = scaled(got[0], [pick(upper, w, 0.0) for w in exps(late, "F")])
            front = add if front is None else plus(front, add)
            if not last:
                add = scaled(got[1], [pick(upper, 0.0, w) for w in exps(late, "B")])
                for odd in range(2):
                    late["F", odd] = late["F", odd] + pick(upper, theirs["F", odd], 0.0)
                    late["B", odd] = late["B", odd] + pick(upper, 0.0, theirs["B", odd])
            else:
                (kept,), mine = read_message(loader(keep_ref, item), 1, parts)
                keep_weights, got_weights = [], []
                for odd in range(2):
                    through = theirs["F", odd] + theirs["B", odd]
                    keep_weights.append(jnp.exp(late["B", odd] + pick(upper, 0.0, through)))
                    got_weights.append(jnp.exp(late["B", odd] + pick(upper, mine["F", odd], 0.0)))
                add = plus(scaled(kept, keep_weights), scaled(got[0], got_weights))
            back = add if back is None else plus(back, add)
        tails = [[None] * 2 for _ in range(members)]
        for member in range(members):
            place(member, item, 0, front)
            tails[member][0] = front.get("diagonal", zero)
            if member < members - 1:
                (state, _), logs = read_message(
                    loader(stacked, where_ref[0] ^ member, item), 2, parts
                )
                front = plus(scaled(front, exps(logs, "F")), state)
        for member in reversed(range(members)):
            place(member, item, 1, back)
            tails[member][1] = back.get("diagonal", zero)
            if member > 0:
                (_, state), logs = read_message(
                    loader(stacked, where_ref[0] ^ member, item), 2, parts
                )
                back = plus(scaled(back, exps(logs, "B")), state)
        if gram:
            for member in range(members):
                slot = where_ref[0] ^ member
                ready[slot, item, pl.ds(2 * DK, TAIL), :] = write_tail(tails[member], None)
    for d in range(members):
        outs[d][...] = ready[d]


def local_kernel(
    items, pairs, where_ref, rate_ref, query_hbm, key_ref, value_ref,
    masked_out, product_out, column_out, query_out, query_sem,
):
    def pair_of(slot):
        return (where_ref[0] ^ (slot // items)) * items + slot % items

    fetches = []
    for slot in range(pairs):
        columns = pl.ds(pl.multiple_of(pair_of(slot) * PAIR, PAIR), PAIR)
        fetches.append(
            pltpu.make_async_copy(
                query_hbm.at[:, :, columns], query_out.at[slot], query_sem.at[slot]
            )
        )
        fetches[-1].start()
    upper = (iota2((GROUP, GROUP), 0) <= iota2((GROUP, GROUP), 1)).astype(BF16)
    lower = iota2((GROUP, GROUP), 0) >= iota2((GROUP, GROUP), 1)
    lower_ones = lower.astype(BF16)
    for fetch in fetches:
        fetch.wait()

    @pl.loop(0, pairs)
    def _(slot):
        pair = pair_of(slot)
        rates = jnp.concatenate([rate_ref[2 * pair + odd] for odd in range(2)], axis=0)
        rates = jnp.concatenate([rates, jnp.zeros((4, GROUP), F32)], axis=0)
        parts = jnp.concatenate(split3(rates) + (jnp.zeros((8, GROUP), F32),), axis=0).astype(BF16)
        sums = dot(parts, upper)
        across = sums[:8] + sums[8:16] + sums[16:24]
        downs = dot_nt(lower_ones, parts)
        down = downs[:, :8] + downs[:, 8:16] + downs[:, 16:24]
        fading = jnp.exp(down)
        raw = {}
        for odd in range(2):
            for row in range(2):
                index = 2 * odd + row
                column_out[slot, index] = jnp.broadcast_to(
                    fading[:, index : index + 1], (GROUP, DK)
                )
                columns = slice(odd * DK, (odd + 1) * DK)
                raw[index] = dot_nt(query_out[slot, row, :, columns], key_ref[slot, row, :, columns])
        scores = {}
        for index in range(4):
            within = jnp.where(
                lower,
                jnp.exp(
                    jnp.minimum(down[:, index : index + 1] - across[index : index + 1, :], 0.0)
                ),
                0.0,
            )
            masked_out[slot, index] = within
            scores[index] = (raw[index] * within).astype(BF16)
        for odd in range(2):
            for row in range(2):
                index = 2 * odd + row
                columns = slice(odd * DK, (odd + 1) * DK)
                both = jnp.concatenate(
                    [key_ref[slot, row, :, columns], value_ref[slot, row, :, columns]], axis=1
                )
                product_out[slot, index] = dot(scores[index], both)


def sum_lanes(x):
    high = x.astype(BF16)
    low = (x - high.astype(F32)).astype(BF16)
    return dot(jnp.concatenate([high, low], axis=1), jnp.ones((2 * x.shape[1], DK), BF16))


def solve_kernel(
    items, pairs, where_ref, ridge_ref, query_ref, key_ref, value_ref, within_ref, product_ref,
    column_ref, gram_ref, solution_out, partial_out,
):
    lower = square_lower()
    diagonal = iota2((DK, DK), 0) == iota2((DK, DK), 1)
    cases = [(row, odd) for row in range(2) for odd in range(2)]
    lanes = [slice(odd * DK, (odd + 1) * DK) for odd in range(2)]

    @pl.loop(0, pairs)
    def _(slot):
        d, item = slot // items, slot % items
        pair = (where_ref[0] ^ d) * items + item
        tails = gram_ref[d, item, pl.ds(2 * DK, TAIL), :].astype(F32)
        grams = {}
        for row in range(2):
            folded = gram_ref[d, item, pl.ds(row * DK, DK), :].astype(F32)
            turned = folded.T
            grams[row, 0] = jnp.where(lower, folded, turned).astype(BF16)
            grams[row, 1] = jnp.where(
                diagonal, tails[row : row + 1], jnp.where(lower, turned, folded)
            ).astype(BF16)

        def entering(row, odd):
            return column_ref[slot, 2 * odd + row]

        def wide(row, odd):
            return query_ref[slot, row, :, lanes[odd]].astype(F32)

        carried = {(r, o): dot(query_ref[slot, r, :, lanes[o]], grams[r, o]) for r, o in cases}
        norm = {(r, o): sum_lanes(wide(r, o) * wide(r, o)) for r, o in cases}
        applied = {
            (r, o): product_ref[slot, 2 * o + r, :, :DK]
            + entering(r, o) * carried[r, o]
            + ridge_ref[2 * pair + o] * wide(r, o)
            for r, o in cases
        }
        curve = {(r, o): sum_lanes(wide(r, o) * applied[r, o]) for r, o in cases}
        size = {case: norm[case] / (curve[case] + solve_epsilon) for case in cases}
        residual = {case: wide(*case) - size[case] * applied[case] for case in cases}
        norm_next = {case: sum_lanes(residual[case] * residual[case]) for case in cases}
        direction = {
            case: (
                residual[case] + norm_next[case] / (norm[case] + solve_epsilon) * wide(*case)
            ).astype(BF16)
            for case in cases
        }
        raw = {(r, o): dot_nt(direction[r, o], key_ref[slot, r, :, lanes[o]]) for r, o in cases}
        carried = {case: dot(direction[case], grams[case]) for case in cases}
        scores = {
            (r, o): (raw[r, o] * within_ref[slot, 2 * o + r]).astype(BF16) for r, o in cases
        }
        second = {
            (r, o): dot(
                scores[r, o],
                jnp.concatenate(
                    [key_ref[slot, r, :, lanes[o]], value_ref[slot, r, :, lanes[o]]], axis=1
                ),
            )
            for r, o in cases
        }
        turn = {case: direction[case].astype(F32) for case in cases}
        applied = {
            (r, o): second[r, o][:, :DK]
            + entering(r, o) * carried[r, o]
            + ridge_ref[2 * pair + o] * turn[r, o]
            for r, o in cases
        }
        curve = {case: sum_lanes(turn[case] * applied[case]) for case in cases}
        for r, o in cases:
            size_next = norm_next[r, o] / (curve[r, o] + solve_epsilon)
            solution_out[slot, r, :, lanes[o]] = (
                size[r, o] * wide(r, o) + size_next * turn[r, o]
            ).astype(BF16)
            partial_out[slot, r, :, lanes[o]] = (
                size[r, o] * product_ref[slot, 2 * o + r, :, DK:]
                + size_next * second[r, o][:, DK:]
            )


def readout_kernel(
    items, pairs, where_ref, column_ref, gain_ref, solution_ref, partial_ref, memory_ref,
    normed_out,
):
    cases = [(row, odd) for row in range(2) for odd in range(2)]
    lanes = [slice(odd * DK, (odd + 1) * DK) for odd in range(2)]
    for slot in range(pairs):
        d, item = slot // items, slot % items
        pair = (where_ref[0] ^ d) * items + item
        readout = {
            (r, o): partial_ref[slot, r, :, lanes[o]]
            + column_ref[slot, 2 * o + r]
            * dot(
                solution_ref[slot, r, :, lanes[o]],
                memory_ref[d, item, pl.ds((2 * r + o) * DK, DK), :],
            )
            for r, o in cases
        }
        square = {case: sum_lanes(readout[case] * readout[case]) for case in cases}
        for r, o in cases:
            columns = pl.ds(pl.multiple_of(pair * PAIR + o * DK, DK), DK)
            scale = lax.rsqrt(square[r, o] * (1.0 / DV) + norm_epsilon)
            normed_out[r, :, columns] = (readout[r, o] * scale * gain_ref[:, columns]).astype(BF16)


def fetch_tiles(weight_hbm, source, columns, held, semaphores):
    depth, width = held.shape[1:]
    rows = pl.ds(pl.multiple_of(source * depth, depth), depth)
    fetches = []
    for tile in range(columns // width):
        fetches.append(
            pltpu.make_async_copy(
                weight_hbm.at[rows, pl.ds(tile * width, width)], held.at[tile], semaphores.at[tile]
            )
        )
        fetches[-1].start()
    return fetches


def own_mix_kernel(sides, side_ref, left_ref, weight_hbm, out_ref, *refs):
    others, (held, semaphores, other_semaphores) = refs[: sides - 1], refs[sides - 1 :]
    width = held.shape[2]
    columns = out_ref.shape[1]
    fetches = fetch_tiles(weight_hbm, side_ref[0], columns, held, semaphores)
    later = []
    for i in range(1, sides):
        source = lax.rem(side_ref[0] + i, sides)
        later += fetch_tiles(weight_hbm, source, columns, others[i - 1], other_semaphores.at[i - 1])
    for tile, fetch in enumerate(fetches):
        fetch.wait()
        out_ref[:, tile * width : (tile + 1) * width] = dot(left_ref[...], held[tile])
    for fetch in later:
        fetch.wait()


def last_mix_kernel(others, own_ref, *refs):
    lefts, rights = refs[:others], refs[others : 2 * others]
    out_hbm, ready, out_semaphores = refs[2 * others :]
    width = ready.shape[2]
    columns = out_hbm.shape[1]
    stores = []
    for tile in range(columns // width):
        lanes = slice(tile * width, (tile + 1) * width)
        total = own_ref[:, lanes]
        for i in range(others):
            total = total + dot(lefts[i][...], rights[i][tile])
        ready[tile] = total.astype(BF16)
        stores.append(
            pltpu.make_async_copy(
                ready.at[tile], out_hbm.at[:, pl.ds(tile * width, width)], out_semaphores.at[tile]
            )
        )
        stores[-1].start()
    for store in stores:
        store.wait()


def whole_blocks(count):
    return [pl.BlockSpec(memory_space=pltpu.VMEM)] * count


def cost(mflops, kib):
    return pl.CostEstimate(
        flops=mflops * 1_000_000, bytes_accessed=kib * 1024, transcendentals=0
    )


def params(limit_mib, dims=None):
    return pltpu.CompilerParams(vmem_limit_bytes=limit_mib * MIB, dimension_semantics=dims)


def on_device(queries, key_vectors, value_vectors, log_decay, ridge_shift, norm_gain, out_weight):
    block = queries.shape[1]
    heads = queries.shape[2] // DK
    pairs = heads // 2
    count = lax.axis_size("ctx")
    members = 1
    while pairs % (2 * members) == 0 and (2 * members) ** 2 <= count:
        members *= 2
    slabs = count // members
    steps = slabs.bit_length() - 1
    items = pairs // members
    mine = lax.axis_index("ctx")
    place = mine % members
    where = jnp.stack([place, mine // members]).astype(jnp.int32)
    smem = pl.BlockSpec(memory_space=pltpu.SMEM)

    def swap(value, distance):
        if distance == 0:
            return value
        return lax.ppermute(value, "ctx", [(i, i ^ distance) for i in range(count)])

    def run(kernel, shapes, scratch, *operands):
        return pl.pallas_call(
            kernel,
            out_shape=[jax.ShapeDtypeStruct(shape, BF16) for shape in shapes],
            in_specs=[smem] + whole_blocks(len(operands)),
            out_specs=whole_blocks(len(shapes)),
            scratch_shapes=[pltpu.VMEM(shape, BF16) for shape in scratch],
            compiler_params=params(12),
        )(where, *operands)

    def in_hbm(*values):
        return [pltpu.with_memory_space_constraint(value, pltpu.HBM) for value in values]

    message = (items, ROWS, DK)
    hbm = pl.BlockSpec(memory_space=pltpu.HBM)
    rows_by_slot = jax.ShapeDtypeStruct((pairs, 2, block, PAIR), BF16)
    *states, keys, values, rates = pl.pallas_call(
        functools.partial(states_kernel, members, items),
        out_shape=[jax.ShapeDtypeStruct(message, BF16)] * members
        + [rows_by_slot] * 2
        + [jax.ShapeDtypeStruct(log_decay.shape, F32)],
        in_specs=[smem, hbm, hbm, hbm],
        out_specs=whole_blocks(members + 3),
        scratch_shapes=[
            pltpu.VMEM((4 * pairs, GROUP), F32),
            pltpu.VMEM((3, 4 * pairs, DK), F32),
            pltpu.SemaphoreType.DMA((pairs,)),
            pltpu.SemaphoreType.DMA((pairs,)),
            pltpu.SemaphoreType.DMA(()),
        ],
        compiler_params=params(16),
        cost_estimate=cost(0, 0),
    )(where, *in_hbm(log_decay, key_vectors, value_vectors))
    slab = [swap(state, d) for d, state in enumerate(states)]

    square = (pairs, 4, GROUP, GROUP)
    within, product, column, query_rows = pl.pallas_call(
        functools.partial(local_kernel, items, pairs),
        out_shape=[
            jax.ShapeDtypeStruct(square, F32),
            jax.ShapeDtypeStruct(square, F32),
            jax.ShapeDtypeStruct((pairs, 4, GROUP, DK), F32),
            rows_by_slot,
        ],
        in_specs=[smem] + whole_blocks(1) + [hbm] + whole_blocks(2),
        out_specs=whole_blocks(4),
        scratch_shapes=[pltpu.SemaphoreType.DMA((pairs,))],
        compiler_params=params(16),
        cost_estimate=cost(4000, 4000),
    )(where, rates, *in_hbm(queries), keys, values)

    def shapes(last):
        return [(items, HALF + TAIL, DK)] * 2 if last else [message]

    bit_next = 0 if steps == 1 else None
    messages = run(
        functools.partial(plane_kernel, members, items, bit_next),
        shapes(steps == 1),
        [(members,) + message],
        *slab,
        column,
    )
    got = []
    for step in range(steps):
        got.append(swap(messages[0], members << step))
        if step == steps - 1:
            break
        last = step == steps - 2
        messages = run(
            functools.partial(step_kernel, items, step, step + 1 if last else None),
            shapes(last),
            [],
            messages[0],
            got[-1],
        )

    def replies(part, rows, after):
        backs = run(
            functools.partial(entering_kernel, (part,), members, items, steps),
            [(items, rows, DK)] * members,
            [(members,) + message, (members, items, rows, DK)],
            *slab,
            *got,
            messages[1],
            after,
        )
        return jnp.stack([swap(back, d) for d, back in enumerate(backs)]), backs[0]

    entering_grams, after = replies("gram", ROWS_G, column)
    entering_memories, _ = replies("memory", ROWS_M, after)

    solution_rows, partial_rows = pl.pallas_call(
        functools.partial(solve_kernel, items, pairs),
        in_specs=[smem, smem] + whole_blocks(7),
        out_specs=whole_blocks(2),
        out_shape=[rows_by_slot, jax.ShapeDtypeStruct(rows_by_slot.shape, F32)],
        compiler_params=params(12),
        cost_estimate=cost(4000, 4000),
    )(
        where, ridge_shift, query_rows, keys, values, within, product, column, entering_grams,
    )
    normed = pl.pallas_call(
        functools.partial(readout_kernel, items, pairs),
        in_specs=[smem] + whole_blocks(5),
        out_specs=whole_blocks(1)[0],
        out_shape=jax.ShapeDtypeStruct(queries.shape, BF16),
        compiler_params=params(16),
    )(
        where, column, norm_gain.reshape(1, -1), solution_rows, partial_rows, entering_memories,
    )

    flattened = normed.reshape(2 * block, heads * DV)
    sides = lax.axis_size("head")
    side = lax.axis_index("head").reshape(1).astype(jnp.int32)
    lefts = [
        lax.ppermute(flattened, "head", [((i + d) % sides, i) for i in range(sides)])
        for d in range(1, sides)
    ]
    columns = out_weight.shape[1]
    width = min(columns, 512)
    tiles = columns // width
    depth = heads * DV
    (weight_in_hbm,) = in_hbm(out_weight)
    held = (tiles, depth, width)
    own, *others = pl.pallas_call(
        functools.partial(own_mix_kernel, sides),
        in_specs=[smem] + whole_blocks(1) + [hbm],
        out_specs=whole_blocks(sides),
        out_shape=[jax.ShapeDtypeStruct((2 * block, columns), F32)]
        + [jax.ShapeDtypeStruct(held, BF16)] * (sides - 1),
        scratch_shapes=[
            pltpu.VMEM(held, BF16),
            pltpu.SemaphoreType.DMA((tiles,)),
            pltpu.SemaphoreType.DMA((sides - 1, tiles)),
        ],
        compiler_params=params(12),
        cost_estimate=cost(2000, 2000),
    )(side, flattened, weight_in_hbm)
    mixed = pl.pallas_call(
        functools.partial(last_mix_kernel, sides - 1),
        in_specs=whole_blocks(2 * sides - 1),
        out_specs=hbm,
        out_shape=jax.ShapeDtypeStruct((2 * block, columns), BF16),
        scratch_shapes=[
            pltpu.VMEM((tiles, 2 * block, width), BF16),
            pltpu.SemaphoreType.DMA((tiles,)),
        ],
        compiler_params=params(12),
    )(own, *lefts, *others)
    return mixed.reshape(2, block, columns)


def solution(mesh):
    return jax.shard_map(
        on_device,
        mesh=mesh,
        in_specs=(
            P(None, "ctx", "head"),
            P(None, "ctx", "head"),
            P(None, "ctx", "head"),
            P("head", None, "ctx"),
            P("head"),
            P("head"),
            P(None, "head"),
        ),
        out_specs=P(None, "ctx", "head"),
        check_vma=False,
    )
```

```python
import functools

import jax
import jax.numpy as jnp
from jax import lax
from jax.experimental import pallas as pl
from jax.experimental.pallas import tpu as pltpu
from jax.sharding import PartitionSpec as P

DK = 128
DV = 128
GROUP = 256
PAIR = 2 * DK
TAIL = 16
HALF = 3 * DK
ROWS = 2 * HALF + TAIL
ROWS_G = 2 * DK + TAIL
ROWS_M = 4 * DK
norm_epsilon = 1e-06
solve_epsilon = 1e-06

F32 = jnp.float32
BF16 = jnp.bfloat16
MIB = 1024 * 1024


def iota2(shape, dim):
    return lax.broadcasted_iota(jnp.int32, shape, dim)


def dot(a, b):
    return lax.dot_general(a, b, (((1,), (0,)), ((), ())), preferred_element_type=F32)


def dot_nt(a, b):
    return lax.dot_general(a, b, (((1,), (1,)), ((), ())), preferred_element_type=F32)


def split3(x):
    high = x.astype(BF16).astype(F32)
    middle = (x - high).astype(BF16).astype(F32)
    low = (x - high - middle).astype(BF16).astype(F32)
    return (high, middle, low)


def square_lower():
    return iota2((DK, DK), 0) >= iota2((DK, DK), 1)


def states_kernel(members, items, where_ref, rate_hbm, key_hbm, value_hbm, *refs):
    outs, (keys_in, values_in, rate_ref) = refs[:members], refs[members : members + 3]
    weight_rows, log_tiles, key_sem, value_sem, rate_sem = refs[members + 3 :]
    rate_fetch = pltpu.make_async_copy(rate_hbm, rate_ref, rate_sem)
    rate_fetch.start()
    pairs = members * items
    place = where_ref[0]

    def pair_of(d, item):
        return (place ^ d) * items + item

    def fetches(slot, pair):
        columns = pl.ds(pl.multiple_of(pair * PAIR, PAIR), PAIR)
        return (
            pltpu.make_async_copy(key_hbm.at[:, :, columns], keys_in.at[slot], key_sem.at[slot]),
            pltpu.make_async_copy(
                value_hbm.at[:, :, columns], values_in.at[slot], value_sem.at[slot]
            ),
        )

    for slot in range(pairs):
        for fetch in fetches(slot, pair_of(slot // items, slot % items)):
            fetch.start()
    rate_fetch.wait()
    rows = 4 * pairs
    rates = jnp.concatenate([rate_ref[h] for h in range(2 * pairs)], axis=0)
    parts = jnp.concatenate(split3(rates), axis=0).astype(BF16)
    upper = (iota2((GROUP, GROUP), 0) <= iota2((GROUP, GROUP), 1)).astype(BF16)
    sums = dot(parts, upper)
    cumulative = sums[:rows] + sums[rows : 2 * rows] + sums[2 * rows :]
    whole = dot(parts, jnp.ones((GROUP, DK), BF16))
    totals = whole[:rows] + whole[rows : 2 * rows] + whole[2 * rows :]
    weight_rows[...] = jnp.exp(
        jnp.minimum(jnp.concatenate([totals, totals], axis=1) - cumulative, 0.0)
    )
    for third, part in enumerate(split3(totals)):
        log_tiles[third] = part
    lower = square_lower()
    diagonal = iota2((DK, DK), 0) == iota2((DK, DK), 1)
    for slot in range(pairs):
        d, item = slot // items, slot % items
        pair = pair_of(d, item)
        for fetch in fetches(slot, pair):
            fetch.wait()
        tail = []
        for row in range(2):
            grams = []
            for odd in range(2):
                index = 4 * pair + 2 * odd + row
                keys = keys_in[slot, row, :, odd * DK : (odd + 1) * DK]
                values = values_in[slot, row, :, odd * DK : (odd + 1) * DK]
                turned = keys.astype(F32).T * weight_rows[pl.ds(index, 1), :]
                product = dot(turned.astype(BF16), jnp.concatenate([keys, values], axis=1))
                grams.append(product[:, :DK])
                start = row * HALF + (1 + odd) * DK
                outs[d][item, pl.ds(start, DK), :] = product[:, DK:].astype(BF16)
            folded = jnp.where(lower, grams[0], grams[1])
            outs[d][item, pl.ds(row * HALF, DK), :] = folded.astype(BF16)
            tail.append(jnp.sum(jnp.where(diagonal, grams[1], 0.0), axis=0, keepdims=True))
        for row in range(2):
            for odd in range(2):
                index = 4 * pair + 2 * odd + row
                tail += [log_tiles[third, pl.ds(index, 1), :] for third in range(3)]
        tail.append(jnp.zeros((2, DK), F32))
        outs[d][item, pl.ds(2 * HALF, TAIL), :] = jnp.concatenate(tail, axis=0).astype(BF16)


def read_tail(block):
    def one(start):
        return block[start : start + 1] + block[start + 1 : start + 2] + block[start + 2 : start + 3]

    logs = {("F", 0): one(2), ("F", 1): one(5), ("B", 0): one(8), ("B", 1): one(11)}
    return (block[0:1], block[1:2]), logs


def read_state(load, start, diagonal, parts):
    state = {}
    if "gram" in parts:
        state["gram"] = load(start, DK)
        state["diagonal"] = diagonal
    if "memory" in parts:
        state["even"] = load(start + DK, DK)
        state["odd"] = load(start + 2 * DK, DK)
    return state


def loader(ref, *lead):
    return lambda start, rows: ref[(*lead, pl.ds(start, rows), slice(None))].astype(F32)


def read_message(load, count, parts):
    diagonals, logs = read_tail(load(count * HALF, TAIL))
    states = [read_state(load, i * HALF, diagonals[i], parts) for i in range(count)]
    return states, logs


def scaled(state, weights):
    out = {}
    for name, value in state.items():
        if name == "gram":
            out[name] = value * jnp.where(square_lower(), weights[0], weights[1])
        else:
            out[name] = value * weights[0 if name == "even" else 1]
    return out


def plus(a, b):
    return {name: a[name] + b[name] for name in a}


def pick(flag, a, b):
    return jnp.where(flag, a, b)


def exps(logs, name):
    return [jnp.exp(logs[name, odd]) for odd in range(2)]


def write_tail(diagonals, logs):
    rows = list(diagonals) + [jnp.zeros((1, DK), F32)] * (2 - len(diagonals))
    for key in (("F", 0), ("F", 1), ("B", 0), ("B", 1)):
        rows += split3(logs[key]) if logs is not None else [jnp.zeros((3, DK), F32)]
    rows.append(jnp.zeros((2, DK), F32))
    return jnp.concatenate(rows, axis=0).astype(BF16)


def write_message(ref, item, states, logs):
    for i, state in enumerate(states):
        for j, name in enumerate(("gram", "even", "odd")):
            ref[item, pl.ds(i * HALF + j * DK, DK), :] = state[name].astype(BF16)
    ref[item, pl.ds(len(states) * HALF, TAIL), :] = write_tail(
        [state["diagonal"] for state in states], logs
    )


BOTH = ("gram", "memory")


def emit(item, front, back, logs, last_bit, outs):
    if last_bit is None:
        write_message(outs[0], item, [front, back], logs)
        return
    upper = last_bit == 1
    weights = [pick(upper, w, 1.0) for w in exps(logs, "B")]
    kept = {name: pick(upper, value, 0.0) for name, value in back.items()}
    write_message(outs[0], item, [plus(scaled(front, weights), kept)], logs)
    write_message(outs[1], item, [front], logs)


def gather_members(members, state_refs, stacked):
    for d in range(members):
        stacked[d] = state_refs[d][...]


def plane_kernel(members, items, bit_next, where_ref, *refs):
    state_refs, outs, stacked = refs[:members], refs[members + 1 : -1], refs[-1]
    gather_members(members, state_refs, stacked)
    last_bit = None if bit_next is None else (where_ref[1] >> bit_next) & 1
    for item in range(items):
        front = back = None
        total = None
        for member in range(members):
            (state, _), logs = read_message(
                loader(stacked, where_ref[0] ^ member, item), 2, BOTH
            )
            front = state if front is None else plus(scaled(front, exps(logs, "F")), state)
            total = logs if total is None else {key: total[key] + logs[key] for key in logs}
        for member in reversed(range(members)):
            (_, state), logs = read_message(
                loader(stacked, where_ref[0] ^ member, item), 2, BOTH
            )
            back = state if back is None else plus(scaled(back, exps(logs, "B")), state)
        emit(item, front, back, total, last_bit, outs)


def step_kernel(items, bit, bit_next, where_ref, own_ref, got_ref, *outs):
    upper = ((where_ref[1] >> bit) & 1) == 1
    last_bit = None if bit_next is None else (where_ref[1] >> bit_next) & 1
    for item in range(items):
        own, mine = read_message(loader(own_ref, item), 2, BOTH)
        got, theirs = read_message(loader(got_ref, item), 2, BOTH)
        sides = []
        for which, name in enumerate(("F", "B")):
            own_first = upper if name == "B" else jnp.logical_not(upper)
            own_weights = [pick(own_first, w, 1.0) for w in exps(theirs, name)]
            got_weights = [pick(own_first, 1.0, w) for w in exps(mine, name)]
            sides.append(plus(scaled(own[which], own_weights), scaled(got[which], got_weights)))
        total = {key: mine[key] + theirs[key] for key in mine}
        emit(item, sides[0], sides[1], total, last_bit, outs)


def entering_kernel(parts, members, items, steps, where_ref, *refs):
    state_refs, got_refs = refs[:members], refs[members : members + steps]
    keep_ref, outs = refs[members + steps], refs[members + steps + 2 : -2]
    stacked, ready = refs[-2:]
    gather_members(members, state_refs, stacked)
    gram, memory = "gram" in parts, "memory" in parts

    def place(member, item, which, state):
        slot = where_ref[0] ^ member
        if gram:
            ready[slot, item, pl.ds(which * DK, DK), :] = state["gram"].astype(BF16)
        if memory:
            for odd, name in enumerate(("even", "odd")):
                start = (2 * which + odd) * DK
                ready[slot, item, pl.ds(start, DK), :] = state[name].astype(BF16)

    for item in range(items):
        zero = jnp.zeros((1, DK), F32)
        late = {key: zero for key in (("F", 0), ("F", 1), ("B", 0), ("B", 1))}
        front = back = None
        for step in range(steps):
            upper = ((where_ref[1] >> step) & 1) == 1
            last = step == steps - 1
            got, theirs = read_message(loader(got_refs[step], item), 1 if last else 2, parts)
            add = scaled(got[0], [pick(upper, w, 0.0) for w in exps(late, "F")])
            front = add if front is None else plus(front, add)
            if not last:
                add = scaled(got[1], [pick(upper, 0.0, w) for w in exps(late, "B")])
                for odd in range(2):
                    late["F", odd] = late["F", odd] + pick(upper, theirs["F", odd], 0.0)
                    late["B", odd] = late["B", odd] + pick(upper, 0.0, theirs["B", odd])
            else:
                (kept,), mine = read_message(loader(keep_ref, item), 1, parts)
                keep_weights, got_weights = [], []
                for odd in range(2):
                    through = theirs["F", odd] + theirs["B", odd]
                    keep_weights.append(jnp.exp(late["B", odd] + pick(upper, 0.0, through)))
                    got_weights.append(jnp.exp(late["B", odd] + pick(upper, mine["F", odd], 0.0)))
                add = plus(scaled(kept, keep_weights), scaled(got[0], got_weights))
            back = add if back is None else plus(back, add)
        tails = [[None] * 2 for _ in range(members)]
        for member in range(members):
            place(member, item, 0, front)
            tails[member][0] = front.get("diagonal", zero)
            if member < members - 1:
                (state, _), logs = read_message(
                    loader(stacked, where_ref[0] ^ member, item), 2, parts
                )
                front = plus(scaled(front, exps(logs, "F")), state)
        for member in reversed(range(members)):
            place(member, item, 1, back)
            tails[member][1] = back.get("diagonal", zero)
            if member > 0:
                (_, state), logs = read_message(
                    loader(stacked, where_ref[0] ^ member, item), 2, parts
                )
                back = plus(scaled(back, exps(logs, "B")), state)
        if gram:
            for member in range(members):
                slot = where_ref[0] ^ member
                ready[slot, item, pl.ds(2 * DK, TAIL), :] = write_tail(tails[member], None)
    for d in range(members):
        outs[d][...] = ready[d]


LANES = [slice(odd * DK, (odd + 1) * DK) for odd in range(2)]


def beside(a, b):
    none = jnp.zeros_like(a)
    return jnp.concatenate(
        [jnp.concatenate([a, none], axis=1), jnp.concatenate([none, b], axis=1)], axis=0
    )


def sum_heads(x):
    ones = jnp.ones((DK, DK), BF16)
    return dot(x.astype(BF16), beside(ones, ones))


def local_kernel(
    items, pairs, where_ref, ridge_ref, rate_ref, query_hbm, key_ref, value_ref,
    masked_out, key_out, value_out, column_out, query_out, query_sem,
):
    def pair_of(slot):
        return (where_ref[0] ^ (slot // items)) * items + slot % items

    fetches = []
    for slot in range(pairs):
        columns = pl.ds(pl.multiple_of(pair_of(slot) * PAIR, PAIR), PAIR)
        fetches.append(
            pltpu.make_async_copy(
                query_hbm.at[:, :, columns], query_out.at[slot], query_sem.at[slot]
            )
        )
        fetches[-1].start()
    upper = (iota2((GROUP, GROUP), 0) <= iota2((GROUP, GROUP), 1)).astype(BF16)
    lower = iota2((GROUP, GROUP), 0) >= iota2((GROUP, GROUP), 1)
    lower_ones = lower.astype(BF16)
    for fetch in fetches:
        fetch.wait()

    @pl.loop(0, pairs)
    def _(slot):
        pair = pair_of(slot)
        rates = jnp.concatenate([rate_ref[2 * pair + odd] for odd in range(2)], axis=0)
        rates = jnp.concatenate([rates, jnp.zeros((4, GROUP), F32)], axis=0)
        parts = jnp.concatenate(split3(rates) + (jnp.zeros((8, GROUP), F32),), axis=0).astype(BF16)
        sums = dot(parts, upper)
        across = sums[:8] + sums[8:16] + sums[16:24]
        downs = dot_nt(lower_ones, parts)
        down = downs[:, :8] + downs[:, 8:16] + downs[:, 16:24]
        fading = jnp.exp(down)
        raw = {}
        for odd in range(2):
            for row in range(2):
                index = 2 * odd + row
                columns = LANES[odd]
                column_out[slot, row, :, columns] = jnp.broadcast_to(
                    fading[:, index : index + 1], (GROUP, DK)
                )
                raw[index] = dot_nt(query_out[slot, row, :, columns], key_ref[slot, row, :, columns])
        scores = {}
        for index in range(4):
            within = jnp.where(
                lower,
                jnp.exp(
                    jnp.minimum(down[:, index : index + 1] - across[index : index + 1, :], 0.0)
                ),
                0.0,
            )
            masked_out[slot, index] = within
            scores[index] = (raw[index] * within).astype(BF16)
        for odd in range(2):
            for row in range(2):
                index = 2 * odd + row
                columns = LANES[odd]
                both = jnp.concatenate(
                    [key_ref[slot, row, :, columns], value_ref[slot, row, :, columns]], axis=1
                )
                product = dot(scores[index], both)
                wide = query_out[slot, row, :, columns].astype(F32)
                key_out[slot, row, :, columns] = product[:, :DK] + ridge_ref[2 * pair + odd] * wide
                value_out[slot, row, :, columns] = product[:, DK:]


def solve_kernel(
    items, pairs, where_ref, ridge_ref, query_ref, key_ref, value_ref, within_ref, local_ref,
    read_ref, column_ref, gram_ref, solution_out, partial_out,
):
    lower = square_lower()
    diagonal = iota2((DK, DK), 0) == iota2((DK, DK), 1)
    both_rows = range(2)

    @pl.loop(0, pairs)
    def _(slot):
        d, item = slot // items, slot % items
        pair = (where_ref[0] ^ d) * items + item
        tails = gram_ref[d, item, pl.ds(2 * DK, TAIL), :].astype(F32)
        grams = []
        for row in both_rows:
            folded = gram_ref[d, item, pl.ds(row * DK, DK), :].astype(F32)
            turned = folded.T
            even = jnp.where(lower, folded, turned).astype(BF16)
            odd = jnp.where(
                diagonal, tails[row : row + 1], jnp.where(lower, turned, folded)
            ).astype(BF16)
            grams.append((even, odd))
        cases = [(row, odd) for row in both_rows for odd in range(2)]
        parts = [slice(0, DK), slice(DK, GROUP)]
        ones = jnp.ones((DK, DK), BF16)

        def at(ref, case):
            return ref[slot, case[0], :, LANES[case[1]]]

        def wide(case):
            return at(query_ref, case).astype(F32)

        def sum_lanes(x):
            return dot(x.astype(BF16), ones)

        carried = {c: dot(at(query_ref, c), grams[c[0]][c[1]]) for c in cases}
        norm = {c: sum_lanes(wide(c) * wide(c)) for c in cases}
        applied = {c: at(local_ref, c) + at(column_ref, c) * carried[c] for c in cases}
        curve = {c: sum_lanes(wide(c) * applied[c]) for c in cases}
        size = {c: norm[c] / (curve[c] + solve_epsilon) for c in cases}
        residual = {c: wide(c) - size[c] * applied[c] for c in cases}
        norm_next = {c: sum_lanes(residual[c] * residual[c]) for c in cases}
        direction = {
            c: (residual[c] + norm_next[c] / (norm[c] + solve_epsilon) * wide(c)).astype(BF16)
            for c in cases
        }
        raw = {
            (c, i): dot_nt(direction[c][part], key_ref[slot, c[0], : part.stop, LANES[c[1]]])
            for c in cases
            for i, part in enumerate(parts)
        }
        carried = {c: dot(direction[c], grams[c[0]][c[1]]) for c in cases}
        scores = {
            (c, i): (
                raw[c, i] * within_ref[slot, 2 * c[1] + c[0], part, : part.stop]
            ).astype(BF16)
            for c in cases
            for i, part in enumerate(parts)
        }
        second = {}
        for c in cases:
            both = jnp.concatenate([at(key_ref, c), at(value_ref, c)], axis=1)
            second[c] = jnp.concatenate(
                [dot(scores[c, i], both[: part.stop]) for i, part in enumerate(parts)], axis=0
            )
        turn = {c: direction[c].astype(F32) for c in cases}
        applied = {
            c: second[c][:, :DK]
            + at(column_ref, c) * carried[c]
            + ridge_ref[2 * pair + c[1]] * turn[c]
            for c in cases
        }
        curve = {c: sum_lanes(turn[c] * applied[c]) for c in cases}
        for c in cases:
            size_next = norm_next[c] / (curve[c] + solve_epsilon)
            solution_out[slot, c[0], :, LANES[c[1]]] = (
                size[c] * wide(c) + size_next * turn[c]
            ).astype(BF16)
            partial_out[slot, c[0], :, LANES[c[1]]] = (
                size[c] * at(read_ref, c) + size_next * second[c][:, DK:]
            )


def readout_kernel(
    items, pairs, where_ref, column_ref, gain_ref, solution_ref, partial_ref, memory_ref,
    normed_out,
):
    for slot in range(pairs):
        d, item = slot // items, slot % items
        pair = (where_ref[0] ^ d) * items + item
        columns = pl.ds(pl.multiple_of(pair * PAIR, PAIR), PAIR)
        for row in range(2):
            memories = [
                memory_ref[d, item, pl.ds((2 * row + odd) * DK, DK), :] for odd in range(2)
            ]
            readout = partial_ref[slot, row] + column_ref[slot, row] * dot(
                solution_ref[slot, row], beside(*memories)
            )
            scale = lax.rsqrt(sum_heads(readout * readout) * (1.0 / DV) + norm_epsilon)
            normed_out[row, :, columns] = (readout * scale * gain_ref[:, columns]).astype(BF16)


def fetch_tiles(weight_hbm, source, held, semaphores):
    tiles, depth, width = held.shape
    rows = pl.ds(pl.multiple_of(source * depth, depth), depth)
    return [
        pltpu.make_async_copy(
            weight_hbm.at[rows, pl.ds(tile * width, width)], held.at[tile], semaphores.at[tile]
        )
        for tile in range(tiles)
    ]


def own_mix_kernel(sides, side_ref, left_ref, weight_hbm, out_ref, *refs):
    others, (held, semaphores, other_semaphores) = refs[: sides - 1], refs[sides - 1 :]
    tiles, _, width = held.shape
    fetches = fetch_tiles(weight_hbm, side_ref[0], held, semaphores)
    for i in range(1, sides):
        source = lax.rem(side_ref[0] + i, sides)
        fetches += fetch_tiles(weight_hbm, source, others[i - 1], other_semaphores.at[i - 1])
    for fetch in fetches[:tiles]:
        fetch.start()
    for tile in range(tiles):
        fetches[tile].wait()
        if tile == 0:
            for fetch in fetches[tiles:]:
                fetch.start()
        out_ref[:, tile * width : (tile + 1) * width] = dot(left_ref[...], held[tile])
    for fetch in fetches[tiles:]:
        fetch.wait()


def last_mix_kernel(others, own_ref, *refs):
    lefts, rights = refs[:others], refs[others : 2 * others]
    out_hbm, ready, out_semaphores = refs[2 * others :]
    width = ready.shape[2]
    columns = out_hbm.shape[1]
    stores = []
    for tile in range(columns // width):
        lanes = slice(tile * width, (tile + 1) * width)
        total = own_ref[:, lanes]
        for i in range(others):
            total = total + dot(lefts[i][...], rights[i][tile])
        ready[tile] = total.astype(BF16)
        stores.append(
            pltpu.make_async_copy(
                ready.at[tile], out_hbm.at[:, pl.ds(tile * width, width)], out_semaphores.at[tile]
            )
        )
        stores[-1].start()
    for store in stores:
        store.wait()


def whole_blocks(count):
    return [pl.BlockSpec(memory_space=pltpu.VMEM)] * count


def cost(mflops, kib):
    return pl.CostEstimate(
        flops=mflops * 1_000_000, bytes_accessed=kib * 1024, transcendentals=0
    )


def params(limit_mib, dims=None):
    return pltpu.CompilerParams(vmem_limit_bytes=limit_mib * MIB, dimension_semantics=dims)


def on_device(queries, key_vectors, value_vectors, log_decay, ridge_shift, norm_gain, out_weight):
    block = queries.shape[1]
    heads = queries.shape[2] // DK
    pairs = heads // 2
    count = lax.axis_size("ctx")
    members = 1
    while pairs % (2 * members) == 0 and (2 * members) ** 2 <= count:
        members *= 2
    slabs = count // members
    steps = slabs.bit_length() - 1
    items = pairs // members
    mine = lax.axis_index("ctx")
    place = mine % members
    where = jnp.stack([place, mine // members]).astype(jnp.int32)
    smem = pl.BlockSpec(memory_space=pltpu.SMEM)

    def swap(value, distance):
        if distance == 0:
            return value
        return lax.ppermute(value, "ctx", [(i, i ^ distance) for i in range(count)])

    def run(kernel, shapes, scratch, *operands):
        return pl.pallas_call(
            kernel,
            out_shape=[jax.ShapeDtypeStruct(shape, BF16) for shape in shapes],
            in_specs=[smem] + whole_blocks(len(operands)),
            out_specs=whole_blocks(len(shapes)),
            scratch_shapes=[pltpu.VMEM(shape, BF16) for shape in scratch],
            compiler_params=params(12),
        )(where, *operands)

    def in_hbm(*values):
        return [pltpu.with_memory_space_constraint(value, pltpu.HBM) for value in values]

    message = (items, ROWS, DK)
    hbm = pl.BlockSpec(memory_space=pltpu.HBM)
    rows_by_slot = jax.ShapeDtypeStruct((pairs, 2, block, PAIR), BF16)
    *states, keys, values, rates = pl.pallas_call(
        functools.partial(states_kernel, members, items),
        out_shape=[jax.ShapeDtypeStruct(message, BF16)] * members
        + [rows_by_slot] * 2
        + [jax.ShapeDtypeStruct(log_decay.shape, F32)],
        in_specs=[smem, hbm, hbm, hbm],
        out_specs=whole_blocks(members + 3),
        scratch_shapes=[
            pltpu.VMEM((4 * pairs, GROUP), F32),
            pltpu.VMEM((3, 4 * pairs, DK), F32),
            pltpu.SemaphoreType.DMA((pairs,)),
            pltpu.SemaphoreType.DMA((pairs,)),
            pltpu.SemaphoreType.DMA(()),
        ],
        compiler_params=params(16),
        cost_estimate=cost(0, 0),
    )(where, *in_hbm(log_decay, key_vectors, value_vectors))
    slab = [swap(state, d) for d, state in enumerate(states)]

    square = (pairs, 4, GROUP, GROUP)
    within, local, read, column, query_rows = pl.pallas_call(
        functools.partial(local_kernel, items, pairs),
        out_shape=[
            jax.ShapeDtypeStruct(square, F32),
            jax.ShapeDtypeStruct(rows_by_slot.shape, F32),
            jax.ShapeDtypeStruct(rows_by_slot.shape, F32),
            jax.ShapeDtypeStruct(rows_by_slot.shape, F32),
            rows_by_slot,
        ],
        in_specs=[smem, smem] + whole_blocks(1) + [hbm] + whole_blocks(2),
        out_specs=whole_blocks(5),
        scratch_shapes=[pltpu.SemaphoreType.DMA((pairs,))],
        compiler_params=params(16),
        cost_estimate=cost(4000, 4000),
    )(where, ridge_shift, rates, *in_hbm(queries), keys, values)

    def shapes(last):
        return [(items, HALF + TAIL, DK)] * 2 if last else [message]

    bit_next = 0 if steps == 1 else None
    messages = run(
        functools.partial(plane_kernel, members, items, bit_next),
        shapes(steps == 1),
        [(members,) + message],
        *slab,
        column,
    )
    got = []
    for step in range(steps):
        got.append(swap(messages[0], members << step))
        if step == steps - 1:
            break
        last = step == steps - 2
        messages = run(
            functools.partial(step_kernel, items, step, step + 1 if last else None),
            shapes(last),
            [],
            messages[0],
            got[-1],
        )

    def replies(part, rows, after):
        backs = run(
            functools.partial(entering_kernel, (part,), members, items, steps),
            [(items, rows, DK)] * members,
            [(members,) + message, (members, items, rows, DK)],
            *slab,
            *got,
            messages[1],
            after,
        )
        return jnp.stack([swap(back, d) for d, back in enumerate(backs)]), backs[0]

    entering_grams, after = replies("gram", ROWS_G, column)
    entering_memories, _ = replies("memory", ROWS_M, after)

    solution_rows, partial_rows = pl.pallas_call(
        functools.partial(solve_kernel, items, pairs),
        in_specs=[smem, smem] + whole_blocks(8),
        out_specs=whole_blocks(2),
        out_shape=[rows_by_slot, jax.ShapeDtypeStruct(rows_by_slot.shape, F32)],
        compiler_params=params(12),
        cost_estimate=cost(4000, 4000),
    )(
        where, ridge_shift, query_rows, keys, values, within, local, read, column,
        entering_grams,
    )
    normed = pl.pallas_call(
        functools.partial(readout_kernel, items, pairs),
        in_specs=[smem] + whole_blocks(5),
        out_specs=whole_blocks(1)[0],
        out_shape=jax.ShapeDtypeStruct(queries.shape, BF16),
        compiler_params=params(16),
    )(
        where, column, norm_gain.reshape(1, -1), solution_rows, partial_rows, entering_memories,
    )

    flattened = normed.reshape(2 * block, heads * DV)
    sides = lax.axis_size("head")
    side = lax.axis_index("head").reshape(1).astype(jnp.int32)
    lefts = [
        lax.ppermute(flattened, "head", [((i + d) % sides, i) for i in range(sides)])
        for d in range(1, sides)
    ]
    columns = out_weight.shape[1]
    width = min(columns, 512)
    tiles = columns // width
    depth = heads * DV
    (weight_in_hbm,) = in_hbm(out_weight)
    held = (tiles, depth, width)
    own, *others = pl.pallas_call(
        functools.partial(own_mix_kernel, sides),
        in_specs=[smem] + whole_blocks(1) + [hbm],
        out_specs=whole_blocks(sides),
        out_shape=[jax.ShapeDtypeStruct((2 * block, columns), F32)]
        + [jax.ShapeDtypeStruct(held, BF16)] * (sides - 1),
        scratch_shapes=[
            pltpu.VMEM(held, BF16),
            pltpu.SemaphoreType.DMA((tiles,)),
            pltpu.SemaphoreType.DMA((sides - 1, tiles)),
        ],
        compiler_params=params(12),
        cost_estimate=cost(2000, 2000),
    )(side, flattened, weight_in_hbm)
    mixed = pl.pallas_call(
        functools.partial(last_mix_kernel, sides - 1),
        in_specs=whole_blocks(2 * sides - 1),
        out_specs=hbm,
        out_shape=jax.ShapeDtypeStruct((2 * block, columns), BF16),
        scratch_shapes=[
            pltpu.VMEM((tiles, 2 * block, width), BF16),
            pltpu.SemaphoreType.DMA((tiles,)),
        ],
        compiler_params=params(12),
    )(own, *lefts, *others)
    return mixed.reshape(2, block, columns)


def solution(mesh):
    return jax.shard_map(
        on_device,
        mesh=mesh,
        in_specs=(
            P(None, "ctx", "head"),
            P(None, "ctx", "head"),
            P(None, "ctx", "head"),
            P("head", None, "ctx"),
            P("head"),
            P("head"),
            P(None, "head"),
        ),
        out_specs=P(None, "ctx", "head"),
        check_vma=False,
    )
```

```python
import functools

import jax
import jax.numpy as jnp
from jax import lax
from jax.experimental import pallas as pl
from jax.experimental.pallas import tpu as pltpu
from jax.sharding import PartitionSpec as P

DK = 128
DV = 128
GROUP = 256
PAIR = 2 * DK
TAIL = 16
HALF = 3 * DK
ROWS = 2 * HALF + TAIL
ROWS_G = 2 * DK + TAIL
ROWS_M = 4 * DK
norm_epsilon = 1e-06
solve_epsilon = 1e-06

F32 = jnp.float32
BF16 = jnp.bfloat16
MIB = 1024 * 1024


def iota2(shape, dim):
    return lax.broadcasted_iota(jnp.int32, shape, dim)


def dot(a, b):
    return lax.dot_general(a, b, (((1,), (0,)), ((), ())), preferred_element_type=F32)


def dot_nt(a, b):
    return lax.dot_general(a, b, (((1,), (1,)), ((), ())), preferred_element_type=F32)


def split3(x):
    high = x.astype(BF16).astype(F32)
    middle = (x - high).astype(BF16).astype(F32)
    low = (x - high - middle).astype(BF16).astype(F32)
    return (high, middle, low)


def square_lower():
    return iota2((DK, DK), 0) >= iota2((DK, DK), 1)


def states_kernel(members, items, where_ref, rate_hbm, key_hbm, value_hbm, *refs):
    outs, (keys_in, values_in, rate_ref) = refs[:members], refs[members : members + 3]
    weight_rows, log_tiles, key_sem, value_sem, rate_sem = refs[members + 3 :]
    rate_fetch = pltpu.make_async_copy(rate_hbm, rate_ref, rate_sem)
    rate_fetch.start()
    pairs = members * items
    place = where_ref[0]

    def pair_of(d, item):
        return (place ^ d) * items + item

    def fetches(slot, pair):
        columns = pl.ds(pl.multiple_of(pair * PAIR, PAIR), PAIR)
        return (
            pltpu.make_async_copy(key_hbm.at[:, :, columns], keys_in.at[slot], key_sem.at[slot]),
            pltpu.make_async_copy(
                value_hbm.at[:, :, columns], values_in.at[slot], value_sem.at[slot]
            ),
        )

    for slot in range(pairs):
        for fetch in fetches(slot, pair_of(slot // items, slot % items)):
            fetch.start()
    rate_fetch.wait()
    rows = 4 * pairs
    rates = jnp.concatenate([rate_ref[h] for h in range(2 * pairs)], axis=0)
    parts = jnp.concatenate(split3(rates), axis=0).astype(BF16)
    upper = (iota2((GROUP, GROUP), 0) <= iota2((GROUP, GROUP), 1)).astype(BF16)
    sums = dot(parts, upper)
    cumulative = sums[:rows] + sums[rows : 2 * rows] + sums[2 * rows :]
    whole = dot(parts, jnp.ones((GROUP, DK), BF16))
    totals = whole[:rows] + whole[rows : 2 * rows] + whole[2 * rows :]
    weight_rows[...] = jnp.exp(
        jnp.minimum(jnp.concatenate([totals, totals], axis=1) - cumulative, 0.0)
    )
    for third, part in enumerate(split3(totals)):
        log_tiles[third] = part
    lower = square_lower()
    diagonal = iota2((DK, DK), 0) == iota2((DK, DK), 1)
    for slot in range(pairs):
        d, item = slot // items, slot % items
        pair = pair_of(d, item)
        for fetch in fetches(slot, pair):
            fetch.wait()
        tail = []
        for row in range(2):
            grams = []
            for odd in range(2):
                index = 4 * pair + 2 * odd + row
                keys = keys_in[slot, row, :, odd * DK : (odd + 1) * DK]
                values = values_in[slot, row, :, odd * DK : (odd + 1) * DK]
                turned = keys.astype(F32).T * weight_rows[pl.ds(index, 1), :]
                product = dot(turned.astype(BF16), jnp.concatenate([keys, values], axis=1))
                grams.append(product[:, :DK])
                start = row * HALF + (1 + odd) * DK
                outs[d][item, pl.ds(start, DK), :] = product[:, DK:].astype(BF16)
            folded = jnp.where(lower, grams[0], grams[1])
            outs[d][item, pl.ds(row * HALF, DK), :] = folded.astype(BF16)
            tail.append(jnp.sum(jnp.where(diagonal, grams[1], 0.0), axis=0, keepdims=True))
        for row in range(2):
            for odd in range(2):
                index = 4 * pair + 2 * odd + row
                tail += [log_tiles[third, pl.ds(index, 1), :] for third in range(3)]
        tail.append(jnp.zeros((2, DK), F32))
        outs[d][item, pl.ds(2 * HALF, TAIL), :] = jnp.concatenate(tail, axis=0).astype(BF16)


def read_tail(block):
    def one(start):
        return block[start : start + 1] + block[start + 1 : start + 2] + block[start + 2 : start + 3]

    logs = {("F", 0): one(2), ("F", 1): one(5), ("B", 0): one(8), ("B", 1): one(11)}
    return (block[0:1], block[1:2]), logs


def read_state(load, start, diagonal, parts):
    state = {}
    if "gram" in parts:
        state["gram"] = load(start, DK)
        state["diagonal"] = diagonal
    if "memory" in parts:
        state["even"] = load(start + DK, DK)
        state["odd"] = load(start + 2 * DK, DK)
    return state


def loader(ref, *lead):
    return lambda start, rows: ref[(*lead, pl.ds(start, rows), slice(None))].astype(F32)


def read_message(load, count, parts):
    diagonals, logs = read_tail(load(count * HALF, TAIL))
    states = [read_state(load, i * HALF, diagonals[i], parts) for i in range(count)]
    return states, logs


def scaled(state, weights):
    out = {}
    for name, value in state.items():
        if name == "gram":
            out[name] = value * jnp.where(square_lower(), weights[0], weights[1])
        else:
            out[name] = value * weights[0 if name == "even" else 1]
    return out


def plus(a, b):
    return {name: a[name] + b[name] for name in a}


def pick(flag, a, b):
    return jnp.where(flag, a, b)


def exps(logs, name):
    return [jnp.exp(logs[name, odd]) for odd in range(2)]


def write_tail(diagonals, logs):
    rows = list(diagonals) + [jnp.zeros((1, DK), F32)] * (2 - len(diagonals))
    for key in (("F", 0), ("F", 1), ("B", 0), ("B", 1)):
        rows += split3(logs[key]) if logs is not None else [jnp.zeros((3, DK), F32)]
    rows.append(jnp.zeros((2, DK), F32))
    return jnp.concatenate(rows, axis=0).astype(BF16)


def write_message(ref, item, states, logs):
    for i, state in enumerate(states):
        for j, name in enumerate(("gram", "even", "odd")):
            ref[item, pl.ds(i * HALF + j * DK, DK), :] = state[name].astype(BF16)
    ref[item, pl.ds(len(states) * HALF, TAIL), :] = write_tail(
        [state["diagonal"] for state in states], logs
    )


BOTH = ("gram", "memory")


def emit(item, front, back, logs, last_bit, outs):
    if last_bit is None:
        write_message(outs[0], item, [front, back], logs)
        return
    upper = last_bit == 1
    weights = [pick(upper, w, 1.0) for w in exps(logs, "B")]
    kept = {name: pick(upper, value, 0.0) for name, value in back.items()}
    write_message(outs[0], item, [plus(scaled(front, weights), kept)], logs)
    write_message(outs[1], item, [front], logs)


def gather_members(members, state_refs, stacked):
    for d in range(members):
        stacked[d] = state_refs[d][...]


def plane_kernel(members, items, bit_next, where_ref, *refs):
    state_refs, outs, stacked = refs[:members], refs[members + 1 : -1], refs[-1]
    gather_members(members, state_refs, stacked)
    last_bit = None if bit_next is None else (where_ref[1] >> bit_next) & 1
    for item in range(items):
        front = back = None
        total = None
        for member in range(members):
            (state, _), logs = read_message(
                loader(stacked, where_ref[0] ^ member, item), 2, BOTH
            )
            front = state if front is None else plus(scaled(front, exps(logs, "F")), state)
            total = logs if total is None else {key: total[key] + logs[key] for key in logs}
        for member in reversed(range(members)):
            (_, state), logs = read_message(
                loader(stacked, where_ref[0] ^ member, item), 2, BOTH
            )
            back = state if back is None else plus(scaled(back, exps(logs, "B")), state)
        emit(item, front, back, total, last_bit, outs)


def step_kernel(items, bit, bit_next, where_ref, own_ref, got_ref, *outs):
    upper = ((where_ref[1] >> bit) & 1) == 1
    last_bit = None if bit_next is None else (where_ref[1] >> bit_next) & 1
    for item in range(items):
        own, mine = read_message(loader(own_ref, item), 2, BOTH)
        got, theirs = read_message(loader(got_ref, item), 2, BOTH)
        sides = []
        for which, name in enumerate(("F", "B")):
            own_first = upper if name == "B" else jnp.logical_not(upper)
            own_weights = [pick(own_first, w, 1.0) for w in exps(theirs, name)]
            got_weights = [pick(own_first, 1.0, w) for w in exps(mine, name)]
            sides.append(plus(scaled(own[which], own_weights), scaled(got[which], got_weights)))
        total = {key: mine[key] + theirs[key] for key in mine}
        emit(item, sides[0], sides[1], total, last_bit, outs)


def entering_kernel(parts, members, items, steps, where_ref, *refs):
    state_refs, got_refs = refs[:members], refs[members : members + steps]
    keep_ref, outs = refs[members + steps], refs[members + steps + 2 : -2]
    stacked, ready = refs[-2:]
    gram, memory = "gram" in parts, "memory" in parts
    spans = [(2 * HALF, TAIL)]
    for half in range(2):
        spans += [(half * HALF, DK)] if gram else []
        spans += [(half * HALF + DK, 2 * DK)] if memory else []
    for d in range(members):
        for start, count in spans:
            stacked[d, :, pl.ds(start, count), :] = state_refs[d][:, pl.ds(start, count), :]

    def place(member, item, which, state):
        slot = where_ref[0] ^ member
        if gram:
            ready[slot, item, pl.ds(which * DK, DK), :] = state["gram"].astype(BF16)
        if memory:
            for odd, name in enumerate(("even", "odd")):
                start = (2 * which + odd) * DK
                ready[slot, item, pl.ds(start, DK), :] = state[name].astype(BF16)

    for item in range(items):
        zero = jnp.zeros((1, DK), F32)
        late = {key: zero for key in (("F", 0), ("F", 1), ("B", 0), ("B", 1))}
        front = back = None
        for step in range(steps):
            upper = ((where_ref[1] >> step) & 1) == 1
            last = step == steps - 1
            got, theirs = read_message(loader(got_refs[step], item), 1 if last else 2, parts)
            add = scaled(got[0], [pick(upper, w, 0.0) for w in exps(late, "F")])
            front = add if front is None else plus(front, add)
            if not last:
                add = scaled(got[1], [pick(upper, 0.0, w) for w in exps(late, "B")])
                for odd in range(2):
                    late["F", odd] = late["F", odd] + pick(upper, theirs["F", odd], 0.0)
                    late["B", odd] = late["B", odd] + pick(upper, 0.0, theirs["B", odd])
            else:
                (kept,), mine = read_message(loader(keep_ref, item), 1, parts)
                keep_weights, got_weights = [], []
                for odd in range(2):
                    through = theirs["F", odd] + theirs["B", odd]
                    keep_weights.append(jnp.exp(late["B", odd] + pick(upper, 0.0, through)))
                    got_weights.append(jnp.exp(late["B", odd] + pick(upper, mine["F", odd], 0.0)))
                add = plus(scaled(kept, keep_weights), scaled(got[0], got_weights))
            back = add if back is None else plus(back, add)
        tails = [[None] * 2 for _ in range(members)]
        for member in range(members):
            place(member, item, 0, front)
            tails[member][0] = front.get("diagonal", zero)
            if member < members - 1:
                (state, _), logs = read_message(
                    loader(stacked, where_ref[0] ^ member, item), 2, parts
                )
                front = plus(scaled(front, exps(logs, "F")), state)
        for member in reversed(range(members)):
            place(member, item, 1, back)
            tails[member][1] = back.get("diagonal", zero)
            if member > 0:
                (_, state), logs = read_message(
                    loader(stacked, where_ref[0] ^ member, item), 2, parts
                )
                back = plus(scaled(back, exps(logs, "B")), state)
        if gram:
            for member in range(members):
                slot = where_ref[0] ^ member
                ready[slot, item, pl.ds(2 * DK, TAIL), :] = write_tail(tails[member], None)
    for d in range(members):
        outs[d][...] = ready[d]


LANES = [slice(odd * DK, (odd + 1) * DK) for odd in range(2)]


def beside(a, b):
    none = jnp.zeros_like(a)
    return jnp.concatenate(
        [jnp.concatenate([a, none], axis=1), jnp.concatenate([none, b], axis=1)], axis=0
    )


def sum_heads(x):
    ones = jnp.ones((DK, DK), BF16)
    return dot(x.astype(BF16), beside(ones, ones))


def local_kernel(
    items, pairs, where_ref, ridge_ref, rate_ref, query_hbm, key_ref, value_ref,
    masked_out, key_out, value_out, column_out, query_out, query_sem,
):
    def pair_of(slot):
        return (where_ref[0] ^ (slot // items)) * items + slot % items

    fetches = []
    for slot in range(pairs):
        columns = pl.ds(pl.multiple_of(pair_of(slot) * PAIR, PAIR), PAIR)
        fetches.append(
            pltpu.make_async_copy(
                query_hbm.at[:, :, columns], query_out.at[slot], query_sem.at[slot]
            )
        )
        fetches[-1].start()
    upper = (iota2((GROUP, GROUP), 0) <= iota2((GROUP, GROUP), 1)).astype(BF16)
    lower = iota2((GROUP, GROUP), 0) >= iota2((GROUP, GROUP), 1)
    lower_ones = lower.astype(BF16)
    for fetch in fetches:
        fetch.wait()

    @pl.loop(0, pairs)
    def _(slot):
        pair = pair_of(slot)
        rates = jnp.concatenate([rate_ref[2 * pair + odd] for odd in range(2)], axis=0)
        rates = jnp.concatenate([rates, jnp.zeros((4, GROUP), F32)], axis=0)
        parts = jnp.concatenate(split3(rates) + (jnp.zeros((8, GROUP), F32),), axis=0).astype(BF16)
        sums = dot(parts, upper)
        across = sums[:8] + sums[8:16] + sums[16:24]
        downs = dot_nt(lower_ones, parts)
        down = downs[:, :8] + downs[:, 8:16] + downs[:, 16:24]
        fading = jnp.exp(down)
        raw = {}
        for odd in range(2):
            for row in range(2):
                index = 2 * odd + row
                columns = LANES[odd]
                column_out[slot, row, :, columns] = jnp.broadcast_to(
                    fading[:, index : index + 1], (GROUP, DK)
                )
                raw[index] = dot_nt(query_out[slot, row, :, columns], key_ref[slot, row, :, columns])
        scores = {}
        for index in range(4):
            within = jnp.where(
                lower,
                jnp.exp(
                    jnp.minimum(down[:, index : index + 1] - across[index : index + 1, :], 0.0)
                ),
                0.0,
            )
            masked_out[slot, index] = within
            scores[index] = (raw[index] * within).astype(BF16)
        for odd in range(2):
            for row in range(2):
                index = 2 * odd + row
                columns = LANES[odd]
                both = jnp.concatenate(
                    [key_ref[slot, row, :, columns], value_ref[slot, row, :, columns]], axis=1
                )
                product = dot(scores[index], both)
                wide = query_out[slot, row, :, columns].astype(F32)
                key_out[slot, row, :, columns] = product[:, :DK] + ridge_ref[2 * pair + odd] * wide
                value_out[slot, row, :, columns] = product[:, DK:]


def solve_kernel(
    items, pairs, where_ref, ridge_ref, query_ref, key_ref, value_ref, within_ref, local_ref,
    read_ref, column_ref, gram_ref, solution_out, partial_out,
):
    lower = square_lower()
    diagonal = iota2((DK, DK), 0) == iota2((DK, DK), 1)
    both_rows = range(2)

    @pl.loop(0, pairs)
    def _(slot):
        d, item = slot // items, slot % items
        pair = (where_ref[0] ^ d) * items + item
        tails = gram_ref[d, item, pl.ds(2 * DK, TAIL), :].astype(F32)
        grams = []
        for row in both_rows:
            folded = gram_ref[d, item, pl.ds(row * DK, DK), :].astype(F32)
            turned = folded.T
            even = jnp.where(lower, folded, turned).astype(BF16)
            odd = jnp.where(
                diagonal, tails[row : row + 1], jnp.where(lower, turned, folded)
            ).astype(BF16)
            grams.append((even, odd))
        cases = [(row, odd) for row in both_rows for odd in range(2)]
        parts = [slice(0, DK), slice(DK, GROUP)]
        ones = jnp.ones((DK, DK), BF16)

        def at(ref, case):
            return ref[slot, case[0], :, LANES[case[1]]]

        def wide(case):
            return at(query_ref, case).astype(F32)

        def sum_lanes(x):
            return dot(x.astype(BF16), ones)

        carried = {c: dot(at(query_ref, c), grams[c[0]][c[1]]) for c in cases}
        norm = {c: sum_lanes(wide(c) * wide(c)) for c in cases}
        applied = {c: at(local_ref, c) + at(column_ref, c) * carried[c] for c in cases}
        curve = {c: sum_lanes(wide(c) * applied[c]) for c in cases}
        size = {c: norm[c] / (curve[c] + solve_epsilon) for c in cases}
        residual = {c: wide(c) - size[c] * applied[c] for c in cases}
        norm_next = {c: sum_lanes(residual[c] * residual[c]) for c in cases}
        direction = {
            c: (residual[c] + norm_next[c] / (norm[c] + solve_epsilon) * wide(c)).astype(BF16)
            for c in cases
        }
        raw = {
            (c, i): dot_nt(direction[c][part], key_ref[slot, c[0], : part.stop, LANES[c[1]]])
            for c in cases
            for i, part in enumerate(parts)
        }
        carried = {c: dot(direction[c], grams[c[0]][c[1]]) for c in cases}
        scores = {
            (c, i): (
                raw[c, i] * within_ref[slot, 2 * c[1] + c[0], part, : part.stop]
            ).astype(BF16)
            for c in cases
            for i, part in enumerate(parts)
        }
        second = {}
        for c in cases:
            both = jnp.concatenate([at(key_ref, c), at(value_ref, c)], axis=1)
            second[c] = jnp.concatenate(
                [dot(scores[c, i], both[: part.stop]) for i, part in enumerate(parts)], axis=0
            )
        turn = {c: direction[c].astype(F32) for c in cases}
        applied = {
            c: second[c][:, :DK]
            + at(column_ref, c) * carried[c]
            + ridge_ref[2 * pair + c[1]] * turn[c]
            for c in cases
        }
        curve = {c: sum_lanes(turn[c] * applied[c]) for c in cases}
        for c in cases:
            size_next = norm_next[c] / (curve[c] + solve_epsilon)
            solution_out[slot, c[0], :, LANES[c[1]]] = (
                size[c] * wide(c) + size_next * turn[c]
            ).astype(BF16)
            partial_out[slot, c[0], :, LANES[c[1]]] = (
                size[c] * at(read_ref, c) + size_next * second[c][:, DK:]
            )


def readout_kernel(
    items, pairs, where_ref, column_ref, gain_ref, solution_ref, partial_ref, memory_ref,
    normed_out,
):
    for slot in range(pairs):
        d, item = slot // items, slot % items
        pair = (where_ref[0] ^ d) * items + item
        columns = pl.ds(pl.multiple_of(pair * PAIR, PAIR), PAIR)
        for row in range(2):
            memories = [
                memory_ref[d, item, pl.ds((2 * row + odd) * DK, DK), :] for odd in range(2)
            ]
            readout = partial_ref[slot, row] + column_ref[slot, row] * dot(
                solution_ref[slot, row], beside(*memories)
            )
            scale = lax.rsqrt(sum_heads(readout * readout) * (1.0 / DV) + norm_epsilon)
            normed_out[row, :, columns] = (readout * scale * gain_ref[:, columns]).astype(BF16)


def fetch_tiles(weight_hbm, source, held, semaphores):
    tiles, depth, width = held.shape
    rows = pl.ds(pl.multiple_of(source * depth, depth), depth)
    return [
        pltpu.make_async_copy(
            weight_hbm.at[rows, pl.ds(tile * width, width)], held.at[tile], semaphores.at[tile]
        )
        for tile in range(tiles)
    ]


def own_mix_kernel(sides, side_ref, left_ref, weight_hbm, out_ref, *refs):
    others, (held, semaphores, other_semaphores) = refs[: sides - 1], refs[sides - 1 :]
    tiles, _, width = held.shape
    fetches = fetch_tiles(weight_hbm, side_ref[0], held, semaphores)
    for i in range(1, sides):
        source = lax.rem(side_ref[0] + i, sides)
        fetches += fetch_tiles(weight_hbm, source, others[i - 1], other_semaphores.at[i - 1])
    for fetch in fetches[:tiles]:
        fetch.start()
    for tile in range(tiles):
        fetches[tile].wait()
        if tile == 0:
            for fetch in fetches[tiles:]:
                fetch.start()
        out_ref[:, tile * width : (tile + 1) * width] = dot(left_ref[...], held[tile])
    for fetch in fetches[tiles:]:
        fetch.wait()


def last_mix_kernel(others, own_ref, *refs):
    lefts, rights = refs[:others], refs[others : 2 * others]
    out_hbm, ready, out_semaphores = refs[2 * others :]
    width = ready.shape[2]
    columns = out_hbm.shape[1]
    stores = []
    for tile in range(columns // width):
        lanes = slice(tile * width, (tile + 1) * width)
        total = own_ref[:, lanes]
        for i in range(others):
            total = total + dot(lefts[i][...], rights[i][tile])
        ready[tile] = total.astype(BF16)
        stores.append(
            pltpu.make_async_copy(
                ready.at[tile], out_hbm.at[:, pl.ds(tile * width, width)], out_semaphores.at[tile]
            )
        )
        stores[-1].start()
    for store in stores:
        store.wait()


def whole_blocks(count):
    return [pl.BlockSpec(memory_space=pltpu.VMEM)] * count


def cost(mflops, kib):
    return pl.CostEstimate(
        flops=mflops * 1_000_000, bytes_accessed=kib * 1024, transcendentals=0
    )


def params(limit_mib, dims=None):
    return pltpu.CompilerParams(vmem_limit_bytes=limit_mib * MIB, dimension_semantics=dims)


def on_device(queries, key_vectors, value_vectors, log_decay, ridge_shift, norm_gain, out_weight):
    block = queries.shape[1]
    heads = queries.shape[2] // DK
    pairs = heads // 2
    count = lax.axis_size("ctx")
    members = 1
    while pairs % (2 * members) == 0 and (2 * members) ** 2 <= count:
        members *= 2
    slabs = count // members
    steps = slabs.bit_length() - 1
    items = pairs // members
    mine = lax.axis_index("ctx")
    place = mine % members
    where = jnp.stack([place, mine // members]).astype(jnp.int32)
    smem = pl.BlockSpec(memory_space=pltpu.SMEM)

    def swap(value, distance):
        if distance == 0:
            return value
        return lax.ppermute(value, "ctx", [(i, i ^ distance) for i in range(count)])

    def run(kernel, shapes, scratch, *operands):
        return pl.pallas_call(
            kernel,
            out_shape=[jax.ShapeDtypeStruct(shape, BF16) for shape in shapes],
            in_specs=[smem] + whole_blocks(len(operands)),
            out_specs=whole_blocks(len(shapes)),
            scratch_shapes=[pltpu.VMEM(shape, BF16) for shape in scratch],
            compiler_params=params(12),
        )(where, *operands)

    def in_hbm(*values):
        return [pltpu.with_memory_space_constraint(value, pltpu.HBM) for value in values]

    message = (items, ROWS, DK)
    hbm = pl.BlockSpec(memory_space=pltpu.HBM)
    rows_by_slot = jax.ShapeDtypeStruct((pairs, 2, block, PAIR), BF16)
    *states, keys, values, rates = pl.pallas_call(
        functools.partial(states_kernel, members, items),
        out_shape=[jax.ShapeDtypeStruct(message, BF16)] * members
        + [rows_by_slot] * 2
        + [jax.ShapeDtypeStruct(log_decay.shape, F32)],
        in_specs=[smem, hbm, hbm, hbm],
        out_specs=whole_blocks(members + 3),
        scratch_shapes=[
            pltpu.VMEM((4 * pairs, GROUP), F32),
            pltpu.VMEM((3, 4 * pairs, DK), F32),
            pltpu.SemaphoreType.DMA((pairs,)),
            pltpu.SemaphoreType.DMA((pairs,)),
            pltpu.SemaphoreType.DMA(()),
        ],
        compiler_params=params(16),
        cost_estimate=cost(0, 0),
    )(where, *in_hbm(log_decay, key_vectors, value_vectors))
    slab = [swap(state, d) for d, state in enumerate(states)]

    square = (pairs, 4, GROUP, GROUP)
    within, local, read, column, query_rows = pl.pallas_call(
        functools.partial(local_kernel, items, pairs),
        out_shape=[
            jax.ShapeDtypeStruct(square, F32),
            jax.ShapeDtypeStruct(rows_by_slot.shape, F32),
            jax.ShapeDtypeStruct(rows_by_slot.shape, F32),
            jax.ShapeDtypeStruct(rows_by_slot.shape, F32),
            rows_by_slot,
        ],
        in_specs=[smem, smem] + whole_blocks(1) + [hbm] + whole_blocks(2),
        out_specs=whole_blocks(5),
        scratch_shapes=[pltpu.SemaphoreType.DMA((pairs,))],
        compiler_params=params(16),
        cost_estimate=cost(4000, 4000),
    )(where, ridge_shift, rates, *in_hbm(queries), keys, values)

    def shapes(last):
        return [(items, HALF + TAIL, DK)] * 2 if last else [message]

    bit_next = 0 if steps == 1 else None
    messages = run(
        functools.partial(plane_kernel, members, items, bit_next),
        shapes(steps == 1),
        [(members,) + message],
        *slab,
        column,
    )
    got = []
    for step in range(steps):
        got.append(swap(messages[0], members << step))
        if step == steps - 1:
            break
        last = step == steps - 2
        messages = run(
            functools.partial(step_kernel, items, step, step + 1 if last else None),
            shapes(last),
            [],
            messages[0],
            got[-1],
        )

    def replies(part, rows, after):
        backs = run(
            functools.partial(entering_kernel, (part,), members, items, steps),
            [(items, rows, DK)] * members,
            [(members,) + message, (members, items, rows, DK)],
            *slab,
            *got,
            messages[1],
            after,
        )
        return jnp.stack([swap(back, d) for d, back in enumerate(backs)]), backs[0]

    entering_grams, after = replies("gram", ROWS_G, column)
    entering_memories, _ = replies("memory", ROWS_M, after)

    solution_rows, partial_rows = pl.pallas_call(
        functools.partial(solve_kernel, items, pairs),
        in_specs=[smem, smem] + whole_blocks(8),
        out_specs=whole_blocks(2),
        out_shape=[rows_by_slot, jax.ShapeDtypeStruct(rows_by_slot.shape, F32)],
        compiler_params=params(12),
        cost_estimate=cost(4000, 4000),
    )(
        where, ridge_shift, query_rows, keys, values, within, local, read, column,
        entering_grams,
    )
    normed = pl.pallas_call(
        functools.partial(readout_kernel, items, pairs),
        in_specs=[smem] + whole_blocks(5),
        out_specs=whole_blocks(1)[0],
        out_shape=jax.ShapeDtypeStruct(queries.shape, BF16),
        compiler_params=params(16),
    )(
        where, column, norm_gain.reshape(1, -1), solution_rows, partial_rows, entering_memories,
    )

    flattened = normed.reshape(2 * block, heads * DV)
    sides = lax.axis_size("head")
    side = lax.axis_index("head").reshape(1).astype(jnp.int32)
    lefts = [
        lax.ppermute(flattened, "head", [((i + d) % sides, i) for i in range(sides)])
        for d in range(1, sides)
    ]
    columns = out_weight.shape[1]
    width = min(columns, 512)
    tiles = columns // width
    depth = heads * DV
    (weight_in_hbm,) = in_hbm(out_weight)
    held = (tiles, depth, width)
    own, *others = pl.pallas_call(
        functools.partial(own_mix_kernel, sides),
        in_specs=[smem] + whole_blocks(1) + [hbm],
        out_specs=whole_blocks(sides),
        out_shape=[jax.ShapeDtypeStruct((2 * block, columns), F32)]
        + [jax.ShapeDtypeStruct(held, BF16)] * (sides - 1),
        scratch_shapes=[
            pltpu.VMEM(held, BF16),
            pltpu.SemaphoreType.DMA((tiles,)),
            pltpu.SemaphoreType.DMA((sides - 1, tiles)),
        ],
        compiler_params=params(12),
        cost_estimate=cost(2000, 2000),
    )(side, flattened, weight_in_hbm)
    mixed = pl.pallas_call(
        functools.partial(last_mix_kernel, sides - 1),
        in_specs=whole_blocks(2 * sides - 1),
        out_specs=hbm,
        out_shape=jax.ShapeDtypeStruct((2 * block, columns), BF16),
        scratch_shapes=[
            pltpu.VMEM((tiles, 2 * block, width), BF16),
            pltpu.SemaphoreType.DMA((tiles,)),
        ],
        compiler_params=params(12),
    )(own, *lefts, *others)
    return mixed.reshape(2, block, columns)


def solution(mesh):
    return jax.shard_map(
        on_device,
        mesh=mesh,
        in_specs=(
            P(None, "ctx", "head"),
            P(None, "ctx", "head"),
            P(None, "ctx", "head"),
            P("head", None, "ctx"),
            P("head"),
            P("head"),
            P(None, "head"),
        ),
        out_specs=P(None, "ctx", "head"),
        check_vma=False,
    )
```
